32 devices in a mesh: car: 2 (over y), branch: 4 (over x, core), pts: 4 (over z).
Axes of the slice: x: 2, y: 2, z: 4, core: 2. Of those that a mesh axis runs over, the one named last changes fastest.
Arguments:
- anchors: bfloat16 [512, 384], P(('car', 'branch', 'pts')), parts along dimension 0, may hold values from -6 to 6
- queries: bfloat16 [4096, 384], P(('car', 'branch', 'pts')), parts along dimension 0, may hold values from -6 to 6
- query_kind: int32 [4096], P(('car', 'branch', 'pts')), parts along dimension 0, may hold values from 0 to 1
- live_count: int32 [32], P(('car', 'branch', 'pts')), parts along dimension 0, may hold values from 16 to 128, as said below
- anchor_gain: float32 [384], replicated, may hold values from 0.25 to 1.75
- query_gain: float32 [384], replicated, may hold values from 0.25 to 1.75
- w_query: bfloat16 [384, 384], replicated, may hold values from -0.3125 to 0.3125
- w_key: bfloat16 [384, 384], replicated, may hold values from -0.3125 to 0.3125
- w_value: bfloat16 [384, 384], replicated, may hold values from -0.3125 to 0.3125
- w_out: bfloat16 [384, 384], replicated, may hold values from -0.3125 to 0.3125
- cotangent: bfloat16 [4096, 384], P(('car', 'branch', 'pts')), parts along dimension 0, may hold values from -6 to 6
Outputs:
- fields: bfloat16 [4096, 384], P(('car', 'branch', 'pts')), parts along dimension 0
- query_grad: float32 [4096, 384], P(('car', 'branch', 'pts')), parts along dimension 0
- anchor_grad: float32 [512, 384], P(('car', 'branch', 'pts')), parts along dimension 0
The draws below stay inside these ranges and needn't reach their ends.
There are 2 independent parts, one for each index of `car`. The reference program is written for one: setup_inputs(seed, part) draws one part's arguments, and reference() takes and returns one part's arrays. A program takes and returns all parts, laid end to end along the dimension named above; an argument that names none is the same for every part. Nothing has to cross between parts.
Inputs may be any that keep to these rules, and one draw needn't show every extreme that they name: `live_count`: each entry counts used slots of one device's 128 slots, the used ones first; some device has all 128 used in every draw.
All inputs are finite; a program needn't handle non-finite values.
Results may differ from the reference program's by a relative error of at most 0.011.
Values may be sent and summed in bfloat16 or wider, within the bound.
No kernel may reach another device: no remote copies, remote signals or barrier semaphores. Data moves between devices by JAX's collectives and lax.ppermute only.
A program may use at most 64 MiB of HBM per device.

```python
import jax
import jax.numpy as jnp
from jax import lax

D = 384
HEADS = 6
QCAP = 128
DEVS = 16
NA = 256
NQ = 2048


def draw_live_count(key, part):
    first_key, second_key = jax.random.split(jax.random.fold_in(key, 17))
    counts = jax.random.randint(first_key, (DEVS,), QCAP // 8, QCAP + 1)
    chosen = jax.random.randint(second_key, (), 0, DEVS)
    return jnp.where(jnp.arange(DEVS) == chosen, QCAP, counts).astype(jnp.int32)


def plant(array, own_key, smallest, top_value):
    shape = array.shape
    index_at = [jax.random.randint(jax.random.fold_in(own_key, axis), (), 0, shape[axis]) for axis in range(len(shape))]
    array = array.at[tuple(index_at)].set(smallest)
    longest = shape.index(max(shape))
    index_at[longest] = (index_at[longest] + 1) % shape[longest]
    return array.at[tuple(index_at)].set(top_value)


def level_of(key, shape, cuts, smallest, high):
    level, own = 1.0, jax.random.fold_in(key, 6)
    for position, blocks in cuts:
        draws = jnp.exp(jax.random.uniform(jax.random.fold_in(own, position), (blocks,), jnp.float32, smallest / len(cuts), high / len(cuts)))
        level = level * jnp.repeat(draws, shape[position] // blocks).reshape([-1 if axis == position else 1 for axis in range(len(shape))])
    return level


def normal_values(own_key, extent, scale, bound, cuts=(), kind=jnp.bfloat16):
    level = level_of(own_key, extent, cuts, -0.22, 0.18) if cuts else 1.0
    array = jax.random.normal(own_key, extent, jnp.float32) * scale * level
    return jnp.minimum(jnp.maximum(array, -bound), bound).astype(kind)


def setup_inputs(seed: int = 0, part: int = 0) -> dict:
    seeds = jax.random.split(jax.random.key(seed), 12)
    own_keys = jax.random.split(jax.random.fold_in(seeds[11], part), 12)
    return {
        "anchors": normal_values(own_keys[0], (NA, D), 1.0, 6.0, ((0, 16),)),
        "queries": normal_values(own_keys[1], (NQ, D), 1.0, 6.0, ((0, 16),)),
        "query_kind": plant(jax.random.randint(own_keys[2], (NQ,), 0, 2), jax.random.fold_in(own_keys[2], 1), 0, 1).astype(jnp.int32),
        "live_count": draw_live_count(jax.random.fold_in(jax.random.fold_in(seeds[11], part), 71), part),
        "anchor_gain": jnp.clip(1.0 + 0.15 * jax.random.normal(seeds[4], (D,), jnp.float32), 0.25, 1.75),
        "query_gain": jnp.clip(1.0 + 0.15 * jax.random.normal(seeds[5], (D,), jnp.float32), 0.25, 1.75),
        "w_query": normal_values(seeds[6], (D, D), D ** -0.5, 0.3125),
        "w_key": normal_values(seeds[7], (D, D), D ** -0.5, 0.3125),
        "w_value": normal_values(seeds[8], (D, D), D ** -0.5, 0.3125),
        "w_out": normal_values(seeds[9], (D, D), D ** -0.5, 0.3125),
        "cotangent": normal_values(own_keys[10], (NQ, D), 1.0, 6.0, ((0, 16),)),
    }


def normed(rows, gain):
    values32 = rows.astype(jnp.float32)
    center = values32 - lax.optimization_barrier(jnp.mean(values32, axis=-1, keepdims=True))
    variance = lax.optimization_barrier(jnp.mean(center * center, axis=-1, keepdims=True))
    return center * lax.rsqrt(variance + 1e-05) * gain

def block_terms(query_heads, kind_rows, live_rows, query_rows, cot_rows, key_rows, value_rows, w_out):
    blocks = query_heads.shape[0]
    anchor_total = key_rows.shape[0]
    head_size = query_heads.shape[1] // HEADS
    score_scale = 1.0 / head_size ** 0.5
    query_split = query_heads.reshape(blocks, HEADS, head_size).astype(jnp.float32)
    key_split = key_rows.reshape(anchor_total, HEADS, head_size).astype(jnp.float32)
    value_split = value_rows.reshape(anchor_total, HEADS, head_size).astype(jnp.float32)
    scores = jnp.einsum('bhd,nhd->hbn', query_split, key_split) * score_scale
    volume_side = jnp.arange(anchor_total) >= anchor_total // 2
    allowed = volume_side[None, :] == (kind_rows[:, None] == 1)
    scores = jnp.where(allowed[None], scores, jnp.float32(-1e+30))
    highest = lax.optimization_barrier(jnp.max(scores, axis=-1, keepdims=True))
    expo = jnp.exp(scores - highest)
    probs = expo / lax.optimization_barrier(jnp.sum(expo, axis=-1, keepdims=True))
    probs_low = probs.astype(jnp.bfloat16)
    mixed = jnp.einsum('hbn,nhd->bhd', probs_low.astype(jnp.float32), value_split)
    mixed = mixed.astype(jnp.bfloat16).reshape(blocks, HEADS * head_size)
    residual = query_rows.astype(jnp.float32) + jnp.dot(mixed, w_out, preferred_element_type=jnp.float32)
    fields = (live_rows[:, None] * residual).astype(jnp.bfloat16)
    grad_rows = (cot_rows.astype(jnp.float32) * live_rows[:, None]).astype(jnp.bfloat16)
    grad_mixed = jnp.dot(grad_rows, w_out.T, preferred_element_type=jnp.float32).astype(jnp.bfloat16)
    grad_split = grad_mixed.reshape(blocks, HEADS, head_size).astype(jnp.float32)
    grad_probs = jnp.einsum('bhd,nhd->hbn', grad_split, value_split)
    row_delta = lax.optimization_barrier(jnp.sum(grad_probs * probs, axis=-1, keepdims=True))
    grad_scores = (probs * (grad_probs - row_delta) * score_scale).astype(jnp.bfloat16)
    grad_scores32 = grad_scores.astype(jnp.float32)
    grad_queries = jnp.einsum('hbn,nhd->bhd', grad_scores32, key_split)
    grad_queries = grad_queries.astype(jnp.bfloat16).reshape(blocks, HEADS * head_size)
    grad_keys = jnp.einsum('hbn,bhd->nhd', grad_scores32, query_split).reshape(anchor_total, HEADS * head_size)
    grad_values = jnp.einsum('hbn,bhd->nhd', probs_low.astype(jnp.float32), grad_split).reshape(anchor_total, HEADS * head_size)
    return (fields, grad_queries, grad_keys, grad_values)

def reference(anchors, queries, query_kind, live_count, anchor_gain, query_gain, w_query, w_key, w_value, w_out, cotangent):
    anchor_normed = normed(anchors, anchor_gain).astype(jnp.bfloat16)
    key_rows = jnp.dot(anchor_normed, w_key, preferred_element_type=jnp.float32).astype(jnp.bfloat16)
    value_rows = jnp.dot(anchor_normed, w_value, preferred_element_type=jnp.float32).astype(jnp.bfloat16)
    query_normed = normed(queries, query_gain).astype(jnp.bfloat16)
    query_heads = jnp.dot(query_normed, w_query, preferred_element_type=jnp.float32).astype(jnp.bfloat16)
    slot_place = jnp.arange(QCAP, dtype=jnp.int32)
    live = (slot_place[None, :] < live_count[:, None]).astype(jnp.float32).reshape(NQ)
    block_rows = 512
    steps_total = NQ // block_rows
    width = query_heads.shape[1]
    stacked = (query_heads.reshape(steps_total, block_rows, width), query_kind.reshape(steps_total, block_rows), live.reshape(steps_total, block_rows), queries.reshape(steps_total, block_rows, width), cotangent.reshape(steps_total, block_rows, width))

    def advance(carry, item):
        fields, grad_queries, grad_keys, grad_values = block_terms(item[0], item[1], item[2], item[3], item[4], key_rows, value_rows, w_out)
        return ((carry[0] + grad_keys, carry[1] + grad_values), (fields, grad_queries))
    start = (jnp.zeros((NA, width), jnp.float32), jnp.zeros((NA, width), jnp.float32))
    sums, outputs = lax.scan(advance, start, stacked)
    fields = outputs[0].reshape(NQ, width)
    grad_queries = outputs[1].reshape(NQ, width)
    grad_normed_q = jnp.dot(grad_queries, w_query.T, preferred_element_type=jnp.float32)
    pullback_q = jax.vjp(lambda rows: normed(rows, query_gain), queries.astype(jnp.float32))[1]
    query_grad = live[:, None] * (cotangent.astype(jnp.float32) + pullback_q(grad_normed_q)[0])
    key_back = w_key.astype(jnp.float32).T
    value_back = w_value.astype(jnp.float32).T
    grad_normed_a = jnp.dot(sums[0], key_back, precision=lax.Precision.HIGHEST)
    grad_normed_a = grad_normed_a + jnp.dot(sums[1], value_back, precision=lax.Precision.HIGHEST)
    pullback_a = jax.vjp(lambda rows: normed(rows, anchor_gain), anchors.astype(jnp.float32))[1]
    anchor_grad = pullback_a(grad_normed_a)[0]
    return (fields, query_grad, anchor_grad)
```

```python
import functools

import jax
import jax.numpy as jnp
from jax import lax
from jax.experimental import pallas as pl
from jax.experimental.pallas import tpu as pltpu
from jax.sharding import PartitionSpec as P

HEADS = 6
GROUP_AXES = ("branch", "pts")

NN = (((1,), (0,)), ((), ()))
NT = (((1,), (1,)), ((), ()))
TN = (((0,), (0,)), ((), ()))


def mm(a, b, dims):
    return lax.dot_general(a, b, dims, preferred_element_type=jnp.float32)


def centered(rows):
    values = rows.astype(jnp.float32)
    center = values - jnp.mean(values, axis=-1, keepdims=True)
    variance = jnp.mean(center * center, axis=-1, keepdims=True)
    return center, lax.rsqrt(variance + 1e-05)


def norm_pullback(center, scale, gain, grad):
    through = grad * gain
    inner = jnp.mean(through * center, axis=-1, keepdims=True)
    grad_center = scale * through - center * (scale * scale * scale * inner)
    return grad_center - jnp.mean(grad_center, axis=-1, keepdims=True)


def live_rows(count, rows):
    return (lax.broadcasted_iota(jnp.int32, (rows, 1), 0) < count).astype(jnp.float32)


def query_side(count, queries, cot, gain, w_query, w_out, heads_out, grad_out):
    center, scale = centered(queries[...])
    query_normed = (center * scale * gain[...]).astype(jnp.bfloat16)
    heads_out[...] = mm(query_normed, w_query[...], NN).astype(jnp.bfloat16)
    live = live_rows(count[0], queries.shape[0])
    grad_rows = (cot[...].astype(jnp.float32) * live).astype(jnp.bfloat16)
    grad_out[...] = mm(grad_rows, w_out[...], NT).astype(jnp.bfloat16)


def attention(ops, place, kind, heads, grads, gain, w_key, w_value, *refs):
    total = len(ops)
    blocks, (own_out, send_out, keep_out, mixed_out, dq_out) = refs[:-5], refs[-5:]
    own, partner, got, other = blocks[0], blocks[1], blocks[2 : 2 + total], blocks[2 + total]
    size = own.shape[0]
    pair = 2 * size
    core, volume = place[0], place[1]

    def slot(k):
        here, there = got[k][...], other[k * pair : (k + 1) * pair, :]
        if ops[k][2]:
            return [jnp.where(core == 0, here, there)]
        return [here, there]

    near, far = [own[...], partner[...]], []
    for k in range(total):
        (far if ops[k][3] else near).extend(slot(k))
    anchors = jnp.concatenate(near + far, 0)
    half = anchors.shape[0] // 2
    center, scale = centered(anchors)
    normed = (center * scale * gain[...]).astype(jnp.bfloat16)
    keys = mm(normed, w_key[...], NN).astype(jnp.bfloat16)
    values = mm(normed, w_value[...], NN).astype(jnp.bfloat16)

    width = keys.shape[1]
    head = width // HEADS
    rows = heads.shape[0]
    score_scale = 1.0 / head**0.5
    lanes = 2 * head
    first = lax.broadcasted_iota(jnp.int32, (1, lanes), 1) < head
    zero = jnp.zeros((), jnp.bfloat16)
    is_near = (kind[...] == 1).astype(jnp.int32) == volume
    is_near = jnp.concatenate([is_near.astype(jnp.int32)] * 2, 1) == 1

    def stack(x):
        return jnp.concatenate([jnp.where(first, x, zero), jnp.where(first, zero, x)], 0)

    def unstack(x):
        return jnp.where(first, x[:rows], x[rows:]).astype(jnp.bfloat16)

    def pick(x):
        return jnp.where(is_near, x[:half], x[half:])

    def spread(x):
        x = x.astype(jnp.float32)
        return jnp.concatenate(
            [jnp.where(is_near, x, 0.0), jnp.where(is_near, 0.0, x)], 0
        ).astype(jnp.bfloat16)

    key_grads, value_grads = [], []
    for at in range(0, width, lanes):
        span = slice(at, at + lanes)
        key, value = keys[:, span], values[:, span]
        query, grad = stack(heads[:, span]), stack(grads[:, span])
        scores = pick(mm(key, query, NT)) * score_scale
        expo = jnp.exp(scores - jnp.max(scores, axis=0, keepdims=True))
        probs = expo / jnp.sum(expo, axis=0, keepdims=True)
        probs_all = spread(probs)
        grad_probs = pick(mm(value, grad, NT))
        delta = jnp.sum(grad_probs * probs, axis=0, keepdims=True)
        grad_scores = spread(probs * (grad_probs - delta) * score_scale)
        mixed_out[:, span] = unstack(mm(probs_all, value, TN))
        dq_out[:, span] = unstack(mm(grad_scores, key, TN))
        key_grads.append(mm(grad_scores, query, NN))
        value_grads.append(mm(probs_all, grad, NN))
    projected = None
    for parts, weight in ((key_grads, w_key), (value_grads, w_value)):
        whole = jnp.concatenate(parts, 1)
        high = whole.astype(jnp.bfloat16)
        low = (whole - high.astype(jnp.float32)).astype(jnp.bfloat16)
        term = mm(high, weight[...], NT) + mm(low, weight[...], NT)
        projected = term if projected is None else projected + term

    own_out[...] = projected[:size]
    send_out[:size, :] = projected[size:pair].astype(jnp.bfloat16)
    starts = {False: pair, True: half}
    for k in range(total):
        at = starts[ops[k][3]]
        here = projected[at : at + pair]
        if ops[k][2]:
            there = jnp.where(core == 0, 0.0, here)
            here = jnp.where(core == 0, here, 0.0)
            starts[ops[k][3]] = at + pair
        else:
            there = projected[at + pair : at + 2 * pair]
            starts[ops[k][3]] = at + 2 * pair
        keep_out[k * pair : (k + 1) * pair, :] = here
        send_out[size + k * pair : size + (k + 1) * pair, :] = there.astype(jnp.bfloat16)


def query_back(count, queries, cot, mixed, dq, gain, w_query, w_out, fields, query_grad):
    live = live_rows(count[0], queries.shape[0])
    residual = queries[...].astype(jnp.float32) + mm(mixed[...], w_out[...], NN)
    fields[...] = (live * residual).astype(jnp.bfloat16)
    center, scale = centered(queries[...])
    back = norm_pullback(center, scale, gain[...], mm(dq[...], w_query[...], NT))
    query_grad[...] = live * (cot[...].astype(jnp.float32) + back)


def add_partner(own, keep, got, own_out, *sums):
    size = own.shape[0]
    pair = 2 * size
    own_out[...] = own[...] + got[:size, :].astype(jnp.float32)
    for k, out in enumerate(sums):
        at = k * pair
        kept = keep[at : at + pair, :]
        out[...] = (kept + got[size + at : size + at + pair, :].astype(jnp.float32)).astype(out.dtype)


def add_chips(*refs):
    got, (own, own_out, send_out) = refs[:-3], refs[-3:]
    size = own.shape[0]
    total = got[0][...].astype(jnp.float32)
    for other in got[1:]:
        total = total + other[...].astype(jnp.float32)
    own_out[...] = own[...] + total[:size]
    send_out[...] = total[size:].astype(send_out.dtype)


def anchor_back(anchors, own, got, gain, out):
    center, scale = centered(anchors[...])
    out[...] = norm_pullback(center, scale, gain[...], own[...] + got[...].astype(jnp.float32))


def call(body, name, outs, scalars, *args):
    specs = [pl.BlockSpec(memory_space=pltpu.SMEM)] * scalars
    specs += [pl.BlockSpec(memory_space=pltpu.VMEM)] * (len(args) - scalars)
    return pl.pallas_call(
        body,
        name=name,
        out_shape=[jax.ShapeDtypeStruct(*out) for out in outs],
        in_specs=specs,
        out_specs=[pl.BlockSpec(memory_space=pltpu.VMEM)] * len(outs),
    )(*args)


def exchange_plan(branches, pts):
    near_bit, top = pts, branches * pts // 2
    plan = []
    for far in (False, True):
        deltas = [d for d in range(branches * pts) if not d & near_bit and bool(d & top) == far and d]
        if len(deltas) % 2:
            plan.append((deltas[-1], None, True, far))
            deltas = deltas[:-1]
        plan.extend((deltas[j], deltas[j + 1], False, far) for j in range(0, len(deltas), 2))
    return plan


def on_device(sizes, anchors, queries, query_kind, live_count, anchor_gain, query_gain, w_query, w_key, w_value, w_out, cotangent):
    branches, pts = sizes
    group = branches * pts
    plan = exchange_plan(branches, pts)
    index = lax.axis_index(GROUP_AXES)

    def swap(x):
        return lax.ppermute(x, GROUP_AXES, [(i, i ^ pts) for i in range(group)])

    def send(x, step):
        pairs = [(i, step[1] if i & pts else step[0]) for i in range(group)]
        return lax.ppermute(x, GROUP_AXES, [(i, i ^ d) for i, d in pairs if d is not None])

    size, width = anchors.shape
    rows = queries.shape[0]
    pair = 2 * size
    f32, bf16 = jnp.float32, jnp.bfloat16
    anchor_gain, query_gain = anchor_gain.reshape(1, -1), query_gain.reshape(1, -1)
    partner = swap(anchors)
    chip = jnp.concatenate([anchors, partner], 0)
    got = [send(chip, step) for step in plan]
    other = swap(jnp.concatenate(got, 0))
    heads, grads = call(
        query_side, "query_side", [((rows, width), bf16)] * 2, 1, live_count, queries, cotangent, query_gain, w_query, w_out
    )
    place = jnp.stack([(index // pts) % 2, (index >= group // 2).astype(jnp.int32)]).astype(jnp.int32)
    own, outgoing, keep, mixed, dq = call(
        functools.partial(attention, plan),
        "attention",
        [
            ((size, width), f32),
            ((size + pair * len(plan), width), bf16),
            ((pair * len(plan), width), f32),
            ((rows, width), bf16),
            ((rows, width), bf16),
        ],
        1,
        place,
        query_kind.reshape(1, -1),
        heads,
        grads,
        anchor_gain,
        w_key,
        w_value,
        anchors,
        partner,
        *got,
        other,
    )
    fields, query_grad = call(
        query_back, "query_back", [((rows, width), bf16), ((rows, width), f32)], 1,
        live_count, queries, cotangent, mixed, dq, query_gain, w_query, w_out,
    )
    own, *sums = call(
        add_partner, "add_partner", [((size, width), f32)] + [((pair, width), bf16)] * len(plan), 0, own, keep, swap(outgoing)
    )
    arrived = [send(part, step) for part, step in zip(sums, plan)]
    own, last = call(add_chips, "add_chips", [((size, width), f32), ((size, width), bf16)], 0, *arrived, own)
    (anchor_grad,) = call(anchor_back, "anchor_back", [((size, width), f32)], 0, anchors, own, swap(last), anchor_gain)
    return fields, query_grad, anchor_grad


def solution(mesh):
    split = P(("car",) + GROUP_AXES, None)
    flat = P(("car",) + GROUP_AXES)
    return jax.shard_map(
        functools.partial(on_device, (mesh.shape["branch"], mesh.shape["pts"])),
        mesh=mesh,
        in_specs=(split, split, flat, flat, P(), P(), P(), P(), P(), P(), split),
        out_specs=(split, split, split),
        check_vma=False,
    )
```

```python
import functools

import jax
import jax.numpy as jnp
from jax import lax
from jax.experimental import pallas as pl
from jax.experimental.pallas import tpu as pltpu
from jax.sharding import PartitionSpec as P

HEADS = 6
GROUP_AXES = ("branch", "pts")

NN = (((1,), (0,)), ((), ()))
NT = (((1,), (1,)), ((), ()))
TN = (((0,), (0,)), ((), ()))


def mm(a, b, dims):
    return lax.dot_general(a, b, dims, preferred_element_type=jnp.float32)


def centered(rows):
    values = rows.astype(jnp.float32)
    center = values - jnp.mean(values, axis=-1, keepdims=True)
    variance = jnp.mean(center * center, axis=-1, keepdims=True)
    return center, lax.rsqrt(variance + 1e-05)


def norm_pullback(center, scale, gain, grad):
    through = grad * gain
    inner = jnp.mean(through * center, axis=-1, keepdims=True)
    grad_center = scale * through - center * (scale * scale * scale * inner)
    return grad_center - jnp.mean(grad_center, axis=-1, keepdims=True)


def as_row(gain):
    return gain[...].reshape(1, -1)


def live_rows(count, rows):
    return (lax.broadcasted_iota(jnp.int32, (rows, 1), 0) < count).astype(jnp.float32)


def query_side(count, queries, cot, gain, w_query, w_out, heads_out, grad_out):
    center, scale = centered(queries[...])
    query_normed = (center * scale * as_row(gain)).astype(jnp.bfloat16)
    heads_out[...] = mm(query_normed, w_query[...], NN).astype(jnp.bfloat16)
    live = live_rows(count[0], queries.shape[0])
    grad_rows = (cot[...].astype(jnp.float32) * live).astype(jnp.bfloat16)
    grad_out[...] = mm(grad_rows, w_out[...], NT).astype(jnp.bfloat16)


def attention(branches, ops, place, kind, heads, grads, gain, w_key, w_value, *refs):
    total = len(ops)
    blocks, (own_out, send_out, keep_out, mixed_out, dq_out) = refs[:-5], refs[-5:]
    own, partner, got, other = blocks[0], blocks[1], blocks[2 : 2 + total], blocks[2 + total]
    size = own.shape[0]
    pair = 2 * size
    core, volume = place[0] % 2, (place[0] >= branches // 2).astype(jnp.int32)

    def slot(k):
        here, there = got[k][...], other[k * pair : (k + 1) * pair, :]
        if ops[k][2]:
            return [jnp.where(core == 0, here, there)]
        return [here, there]

    near, far = [own[...], partner[...]], []
    for k in range(total):
        (far if ops[k][3] else near).extend(slot(k))
    anchors = jnp.concatenate(near + far, 0)
    half = anchors.shape[0] // 2
    center, scale = centered(anchors)
    normed = (center * scale * as_row(gain)).astype(jnp.bfloat16)
    keys = mm(normed, w_key[...], NN).astype(jnp.bfloat16)
    values = mm(normed, w_value[...], NN).astype(jnp.bfloat16)

    width = keys.shape[1]
    head = width // HEADS
    rows = heads.shape[0]
    score_scale = 1.0 / head**0.5
    lanes = 2 * head
    first = lax.broadcasted_iota(jnp.int32, (1, lanes), 1) < head
    zero = jnp.zeros((), jnp.bfloat16)
    is_near = (kind[...] == 1).astype(jnp.int32) == volume
    is_near = jnp.concatenate([is_near.astype(jnp.int32)] * 2, 1) == 1

    def stack(x):
        return jnp.concatenate([jnp.where(first, x, zero), jnp.where(first, zero, x)], 0)

    def unstack(x):
        return jnp.where(first, x[:rows], x[rows:]).astype(jnp.bfloat16)

    def pick(x):
        return jnp.where(is_near, x[:half], x[half:])

    def spread(x):
        x = x.astype(jnp.float32)
        return jnp.concatenate(
            [jnp.where(is_near, x, 0.0), jnp.where(is_near, 0.0, x)], 0
        ).astype(jnp.bfloat16)

    key_grads, value_grads = [], []
    for at in range(0, width, lanes):
        span = slice(at, at + lanes)
        key, value = keys[:, span], values[:, span]
        query, grad = stack(heads[:, span]), stack(grads[:, span])
        scores = pick(mm(key, query, NT)) * score_scale
        expo = jnp.exp(scores - jnp.max(scores, axis=0, keepdims=True))
        probs = expo / jnp.sum(expo, axis=0, keepdims=True)
        probs_all = spread(probs)
        grad_probs = pick(mm(value, grad, NT))
        delta = jnp.sum(grad_probs * probs, axis=0, keepdims=True)
        grad_scores = spread(probs * (grad_probs - delta) * score_scale)
        mixed_out[:, span] = unstack(mm(probs_all, value, TN))
        dq_out[:, span] = unstack(mm(grad_scores, key, TN))
        key_grads.append(mm(grad_scores, query, NN))
        value_grads.append(mm(probs_all, grad, NN))
    projected = None
    for parts, weight in ((key_grads, w_key), (value_grads, w_value)):
        whole = jnp.concatenate(parts, 1)
        high = whole.astype(jnp.bfloat16)
        low = (whole - high.astype(jnp.float32)).astype(jnp.bfloat16)
        term = mm(high, weight[...], NT) + mm(low, weight[...], NT)
        projected = term if projected is None else projected + term

    own_out[...] = projected[:size]
    send_out[:size, :] = projected[size:pair].astype(jnp.bfloat16)
    starts = {False: pair, True: half}
    for k in range(total):
        at = starts[ops[k][3]]
        here = projected[at : at + pair]
        if ops[k][2]:
            there = jnp.where(core == 0, 0.0, here)
            here = jnp.where(core == 0, here, 0.0)
            starts[ops[k][3]] = at + pair
        else:
            there = projected[at + pair : at + 2 * pair]
            starts[ops[k][3]] = at + 2 * pair
        keep_out[k * pair : (k + 1) * pair, :] = here
        send_out[size + k * pair : size + (k + 1) * pair, :] = there.astype(jnp.bfloat16)


def query_back(count, queries, cot, mixed, dq, gain, w_query, w_out, fields, query_grad):
    live = live_rows(count[0], queries.shape[0])
    residual = queries[...].astype(jnp.float32) + mm(mixed[...], w_out[...], NN)
    fields[...] = (live * residual).astype(jnp.bfloat16)
    center, scale = centered(queries[...])
    back = norm_pullback(center, scale, as_row(gain), mm(dq[...], w_query[...], NT))
    query_grad[...] = live * (cot[...].astype(jnp.float32) + back)


def add_partner(own, keep, got, own_out, *sums):
    size = own.shape[0]
    pair = 2 * size
    own_out[...] = own[...] + got[:size, :].astype(jnp.float32)
    for k, out in enumerate(sums):
        at = k * pair
        kept = keep[at : at + pair, :]
        out[...] = (kept + got[size + at : size + at + pair, :].astype(jnp.float32)).astype(out.dtype)


def add_chips(*refs):
    got, (own, own_out, send_out) = refs[:-3], refs[-3:]
    size = own.shape[0]
    total = got[0][...].astype(jnp.float32)
    for other in got[1:]:
        total = total + other[...].astype(jnp.float32)
    own_out[...] = own[...] + total[:size]
    send_out[...] = total[size:].astype(send_out.dtype)


def anchor_back(anchors, own, got, gain, out):
    center, scale = centered(anchors[...])
    out[...] = norm_pullback(center, scale, as_row(gain), own[...] + got[...].astype(jnp.float32))


def call(body, name, outs, scalars, *args):
    specs = [pl.BlockSpec(memory_space=pltpu.SMEM)] * scalars
    specs += [pl.BlockSpec(memory_space=pltpu.VMEM)] * (len(args) - scalars)
    placed = [pltpu.with_memory_space_constraint(x, pltpu.VMEM) for x in args[scalars:]]
    return pl.pallas_call(
        body,
        name=name,
        out_shape=[pltpu.VMEM(*out) if on_chip else jax.ShapeDtypeStruct(*out) for on_chip, *out in outs],
        in_specs=specs,
        out_specs=[pl.BlockSpec(memory_space=pltpu.VMEM)] * len(outs),
        compiler_params=pltpu.CompilerParams(vmem_limit_bytes=32 * 2**20),
    )(*args[:scalars], *placed)


def exchange_plan(branches, pts):
    near_bit, top = pts, branches * pts // 2
    plan = []
    for far in (False, True):
        deltas = [d for d in range(branches * pts) if not d & near_bit and bool(d & top) == far and d]
        if len(deltas) % 2:
            plan.append((deltas[-1], None, True, far))
            deltas = deltas[:-1]
        plan.extend((deltas[j], deltas[j + 1], False, far) for j in range(0, len(deltas), 2))
    return plan


def on_device(sizes, anchors, queries, query_kind, live_count, anchor_gain, query_gain, w_query, w_key, w_value, w_out, cotangent):
    branches, pts = sizes
    group = branches * pts
    plan = exchange_plan(branches, pts)

    def swap(x):
        return lax.ppermute(x, GROUP_AXES, [(i, i ^ pts) for i in range(group)])

    def send(x, step):
        pairs = [(i, step[1] if i & pts else step[0]) for i in range(group)]
        return lax.ppermute(x, GROUP_AXES, [(i, i ^ d) for i, d in pairs if d is not None])

    size, width = anchors.shape
    rows = queries.shape[0]
    pair = 2 * size
    f32, bf16 = jnp.float32, jnp.bfloat16
    partner = swap(anchors)
    chip = jnp.concatenate([anchors, partner], 0)
    got = [send(chip, step) for step in plan]
    other = swap(jnp.concatenate(got, 0))
    heads, grads = call(
        query_side, "query_side", [(True, (rows, width), bf16)] * 2, 1, live_count, queries, cotangent, query_gain, w_query, w_out
    )
    place = lax.axis_index("branch").reshape(1)
    own, outgoing, keep, mixed, dq = call(
        functools.partial(attention, branches, plan),
        "attention",
        [
            (True, (size, width), f32),
            (True, (size + pair * len(plan), width), bf16),
            (True, (pair * len(plan), width), f32),
            (True, (rows, width), bf16),
            (True, (rows, width), bf16),
        ],
        1,
        place,
        query_kind.reshape(1, -1),
        heads,
        grads,
        anchor_gain,
        w_key,
        w_value,
        anchors,
        partner,
        *got,
        other,
    )
    fields, query_grad = call(
        query_back, "query_back", [(False, (rows, width), bf16), (False, (rows, width), f32)], 1,
        live_count, queries, cotangent, mixed, dq, query_gain, w_query, w_out,
    )
    own, *sums = call(
        add_partner, "add_partner", [(True, (size, width), f32)] + [(True, (pair, width), bf16)] * len(plan), 0, own, keep, swap(outgoing)
    )
    arrived = [send(part, step) for part, step in zip(sums, plan)]
    own, last = call(add_chips, "add_chips", [(True, (size, width), f32), (True, (size, width), bf16)], 0, *arrived, own)
    (anchor_grad,) = call(anchor_back, "anchor_back", [(False, (size, width), f32)], 0, anchors, own, swap(last), anchor_gain)
    return fields, query_grad, anchor_grad


def solution(mesh):
    split = P(("car",) + GROUP_AXES, None)
    flat = P(("car",) + GROUP_AXES)
    return jax.shard_map(
        functools.partial(on_device, (mesh.shape["branch"], mesh.shape["pts"])),
        mesh=mesh,
        in_specs=(split, split, flat, flat, P(), P(), P(), P(), P(), P(), split),
        out_specs=(split, split, split),
        check_vma=False,
    )
```

```python
import functools

import jax
import jax.numpy as jnp
from jax import lax
from jax.experimental import pallas as pl
from jax.experimental.pallas import tpu as pltpu
from jax.sharding import PartitionSpec as P


HEADS = 6
GROUP_AXES = ("branch", "pts")

NN = (((1,), (0,)), ((), ()))
NT = (((1,), (1,)), ((), ()))
TN = (((0,), (0,)), ((), ()))


def mm(a, b, dims):
    return lax.dot_general(a, b, dims, preferred_element_type=jnp.float32)


def centered(rows):
    values = rows.astype(jnp.float32)
    center = values - jnp.mean(values, axis=-1, keepdims=True)
    variance = jnp.mean(center * center, axis=-1, keepdims=True)
    return center, lax.rsqrt(variance + 1e-05)


def norm_pullback(center, scale, gain, grad):
    through = grad * gain
    inner = jnp.mean(through * center, axis=-1, keepdims=True)
    grad_center = scale * through - center * (scale * scale * scale * inner)
    return grad_center - jnp.mean(grad_center, axis=-1, keepdims=True)


def as_row(gain):
    return gain[...].reshape(1, -1)


def live_rows(count, rows):
    return (lax.broadcasted_iota(jnp.int32, (rows, 1), 0) < count).astype(jnp.float32)


def query_side(*refs):
    total = (len(refs) - 5) // 2
    sources, outs, count, sems = refs[: total + 1], refs[total + 1 : -2], refs[-2], refs[-1]
    (heads_out, grad_out, live_out), kept = outs[:3], outs[3:]
    copies = [pltpu.make_async_copy(a, b, sems.at[k]) for k, (a, b) in enumerate(zip(sources, kept + (count,)))]
    for copy in copies:
        copy.start()
    queries, cot, gain, w_query, w_out = kept[:5]
    for k in (0, 2):
        copies[k].wait()
    center, scale = centered(queries[...])
    query_normed = (center * scale * as_row(gain)).astype(jnp.bfloat16)
    copies[3].wait()
    heads_out[...] = mm(query_normed, w_query[...], NN).astype(jnp.bfloat16)
    copies[total].wait()
    live = live_rows(count[0, 0], queries.shape[0])
    live_out[...] = live
    copies[1].wait()
    grad_rows = (cot[...].astype(jnp.float32) * live).astype(jnp.bfloat16)
    copies[4].wait()
    grad_out[...] = mm(grad_rows, w_out[...], NT).astype(jnp.bfloat16)
    for copy in copies[5:total]:
        copy.wait()


def join(own, partner, out):
    out[: own.shape[0], :] = own[...]
    out[own.shape[0] :, :] = partner[...]


def attention(ops, kind, heads, grads, gain, w_key, w_value, *refs):
    total = len(ops)
    blocks, (own_out, send_out, keep_out, mixed_out, dq_out) = refs[:-5], refs[-5:]
    own, partner, across, got, other = blocks[0], blocks[1], blocks[2], blocks[3 : 3 + total], blocks[3 + total]
    size = own.shape[0]
    pair = 2 * size
    branch = lax.axis_index("branch")
    core, volume = branch % 2, (branch >= lax.axis_size("branch") // 2).astype(jnp.int32)

    def ordered(first, second):
        return jnp.where(core == 0, first, second), jnp.where(core == 0, second, first)

    sides = ([own[...], partner[...]], [across[...], other[:size, :]])
    for k, (_, _, near, far) in enumerate(ops):
        at = size + k * pair
        here, there = got[k][...], other[at : at + pair, :]
        if near != far:
            here, there = ordered(here, there)
        sides[near].append(here)
        sides[far].append(there)
    anchors = jnp.concatenate(sides[0] + sides[1], 0)
    half = anchors.shape[0] // 2
    center, scale = centered(anchors)
    normed = (center * scale * as_row(gain)).astype(jnp.bfloat16)
    keys = mm(normed, w_key[...], NN).astype(jnp.bfloat16)
    values = mm(normed, w_value[...], NN).astype(jnp.bfloat16)

    width = keys.shape[1]
    head = width // HEADS
    rows = heads.shape[0]
    score_scale = 1.0 / head**0.5
    lanes = 2 * head
    first = lax.broadcasted_iota(jnp.int32, (1, lanes), 1) < head
    zero = jnp.zeros((), jnp.bfloat16)
    is_near = (kind[...] == 1).astype(jnp.int32) == volume
    is_near = jnp.concatenate([is_near.astype(jnp.int32)] * 2, 1) == 1

    def stack(x):
        return jnp.concatenate([jnp.where(first, x, zero), jnp.where(first, zero, x)], 0)

    def unstack(x):
        return jnp.where(first, x[:rows], x[rows:]).astype(jnp.bfloat16)

    def pick(x):
        return jnp.where(is_near, x[:half], x[half:])

    def spread(x):
        x = x.astype(jnp.float32)
        return jnp.concatenate(
            [jnp.where(is_near, x, 0.0), jnp.where(is_near, 0.0, x)], 0
        ).astype(jnp.bfloat16)

    key_grads, value_grads = [], []
    for at in range(0, width, lanes):
        span = slice(at, at + lanes)
        key, value = keys[:, span], values[:, span]
        query, grad = stack(heads[:, span]), stack(grads[:, span])
        scores = pick(mm(key, query, NT)) * score_scale
        expo = jnp.exp(scores - jnp.max(scores, axis=0, keepdims=True))
        probs = expo / jnp.sum(expo, axis=0, keepdims=True)
        probs_all = spread(probs)
        grad_probs = pick(mm(value, grad, NT))
        delta = jnp.sum(grad_probs * probs, axis=0, keepdims=True)
        grad_scores = spread(probs * (grad_probs - delta) * score_scale)
        mixed_out[:, span] = unstack(mm(probs_all, value, TN))
        dq_out[:, span] = unstack(mm(grad_scores, key, TN))
        key_grads.append(mm(grad_scores, query, NN))
        value_grads.append(mm(probs_all, grad, NN))
    projected = None
    for parts, weight in ((key_grads, w_key), (value_grads, w_value)):
        whole = jnp.concatenate(parts, 1)
        high = whole.astype(jnp.bfloat16)
        low = (whole - high.astype(jnp.float32)).astype(jnp.bfloat16)
        term = mm(high, weight[...], NT) + mm(low, weight[...], NT)
        projected = term if projected is None else projected + term

    own_out[...] = projected[:size]
    send_out[:size, :] = projected[size:pair].astype(jnp.bfloat16)
    keep_out[:size, :] = projected[half : half + size]
    send_out[size:pair, :] = projected[half + size : half + pair].astype(jnp.bfloat16)
    starts = [pair, half + pair]

    def take(side):
        at = starts[side]
        starts[side] = at + pair
        return projected[at : at + pair]

    for k, (_, _, near, far) in enumerate(ops):
        here, there = take(near), take(far)
        if near != far:
            here, there = ordered(here, there)
        keep_out[size + k * pair : size + (k + 1) * pair, :] = here
        send_out[pair + k * pair : pair + (k + 1) * pair, :] = there.astype(jnp.bfloat16)


def query_back(live, queries, cot, mixed, dq, gain, w_query, w_out, fields, query_grad):
    residual = queries[...].astype(jnp.float32) + mm(mixed[...], w_out[...], NN)
    fields[...] = (live[...] * residual).astype(jnp.bfloat16)
    center, scale = centered(queries[...])
    back = norm_pullback(center, scale, as_row(gain), mm(dq[...], w_query[...], NT))
    query_grad[...] = live[...] * (cot[...].astype(jnp.float32) + back)


def add_partner(own, keep, got, own_out, across, *sums):
    size = own.shape[0]
    pair = 2 * size
    own_out[...] = own[...] + got[:size, :].astype(jnp.float32)
    across[...] = (keep[:size, :] + got[size:pair, :].astype(jnp.float32)).astype(across.dtype)
    for k, out in enumerate(sums):
        at = size + k * pair
        kept = keep[at : at + pair, :]
        out[...] = (kept + got[size + at : size + at + pair, :].astype(jnp.float32)).astype(out.dtype)


def add_chips(*refs):
    got, (own, own_out, send_out) = refs[:-3], refs[-3:]
    size = own.shape[0]
    total = got[0][...].astype(jnp.float32)
    for other in got[1:]:
        total = total + other[...].astype(jnp.float32)
    own_out[...] = own[...] + total[:size]
    send_out[...] = total[size:].astype(send_out.dtype)


def anchor_back(anchors, own, got, across, gain, out):
    center, scale = centered(anchors[...])
    grad = own[...] + got[...].astype(jnp.float32) + across[...].astype(jnp.float32)
    out[...] = norm_pullback(center, scale, as_row(gain), grad)


def call(body, outs, *args, staged=()):
    specs = [pl.BlockSpec(memory_space=pltpu.VMEM)] * len(args)
    placed = [pltpu.with_memory_space_constraint(x, pltpu.VMEM) for x in args]
    held = [x if x.size == 1 else pltpu.with_memory_space_constraint(x, pltpu.HBM) for x in staged]
    return pl.pallas_call(
        body,
        out_shape=[pltpu.VMEM(*out) if on_chip else jax.ShapeDtypeStruct(*out) for on_chip, *out in outs],
        in_specs=specs + [pl.BlockSpec(memory_space=pl.ANY if x.size == 1 else pltpu.HBM) for x in staged],
        out_specs=[pl.BlockSpec(memory_space=pltpu.VMEM)] * len(outs),
        scratch_shapes=[pltpu.SMEM((1, 1), jnp.int32), pltpu.SemaphoreType.DMA((len(held),))] if held else [],
        compiler_params=pltpu.CompilerParams(vmem_limit_bytes=32 * 2**20),
    )(*placed, *held)


def exchange_plan(branches, pts):
    near_bit, top = pts, branches * pts // 2
    nears = [d for d in range(1, top) if not d & near_bit]
    plan = [(d, d | top) for d in reversed(nears)]
    return [(a, b, int(a >= top), int(b >= top)) for a, b in plan]


def on_device(sizes, anchors, queries, query_kind, live_count, anchor_gain, query_gain, w_query, w_key, w_value, w_out, cotangent):
    branches, pts = sizes
    group = branches * pts
    plan = exchange_plan(branches, pts)

    def send(x, deltas):
        return lax.ppermute(x, GROUP_AXES, [(i, i ^ deltas[(i // pts) % 2]) for i in range(group)])

    def swap(x):
        return send(x, (pts, pts))

    def cross(x):
        return send(x, (group // 2, group // 2))

    size, width = anchors.shape
    rows = queries.shape[0]
    pair = 2 * size
    f32, bf16 = jnp.float32, jnp.bfloat16
    partner = swap(anchors)
    across = cross(anchors)
    (chip,) = call(join, [(True, (pair, width), bf16)], anchors, partner)
    got = []
    for step in plan:
        got.append(send(chip, step))
    inputs = (queries, cotangent, query_gain, w_query, w_out, anchors, anchor_gain, w_key, w_value, query_kind.reshape(1, -1))
    (heads, grads, live, queries, cotangent, query_gain, w_query, w_out, anchors, anchor_gain, w_key, w_value, query_kind) = call(
        query_side,
        [(True, (rows, width), bf16)] * 2 + [(True, (rows, 1), f32)] + [(True, x.shape, x.dtype) for x in inputs],
        staged=inputs + (live_count.reshape(1, 1),),
    )
    other = swap(jnp.concatenate([across] + got, 0))
    own, outgoing, keep, mixed, dq = call(
        functools.partial(attention, plan),
        [
            (True, (size, width), f32),
            (True, (pair + pair * len(plan), width), bf16),
            (True, (size + pair * len(plan), width), f32),
            (True, (rows, width), bf16),
            (True, (rows, width), bf16),
        ],
        query_kind,
        heads,
        grads,
        anchor_gain,
        w_key,
        w_value,
        anchors,
        partner,
        across,
        *got,
        other,
    )
    fields, query_grad = call(
        query_back, [(False, (rows, width), bf16), (False, (rows, width), f32)],
        live, queries, cotangent, mixed, dq, query_gain, w_query, w_out,
    )
    incoming = swap(outgoing)
    own, across, *sums = call(
        add_partner,
        [(True, (size, width), f32), (True, (size, width), bf16)] + [(True, (pair, width), bf16)] * len(plan),
        own,
        keep,
        incoming,
    )
    arrived = []
    for part, step in zip(sums, plan):
        arrived.append(send(part, step))
    across = cross(across)
    own, last = call(add_chips, [(True, (size, width), f32), (True, (size, width), bf16)], *arrived, own)
    last = swap(last)
    (anchor_grad,) = call(anchor_back, [(False, (size, width), f32)], anchors, own, last, across, anchor_gain)
    return fields, query_grad, anchor_grad


def solution(mesh):
    split = P(("car",) + GROUP_AXES, None)
    flat = P(("car",) + GROUP_AXES)
    sizes = mesh.shape["branch"], mesh.shape["pts"]

    def body(*args):
        return on_device(sizes, *args)

    return jax.shard_map(
        body,
        mesh=mesh,
        in_specs=(split, split, flat, flat, P(), P(), P(), P(), P(), P(), split),
        out_specs=(split, split, split),
        check_vma=False,
    )
```

```python
import functools

import jax
import jax.numpy as jnp
from jax import lax
from jax.experimental import pallas as pl
from jax.experimental.pallas import tpu as pltpu
from jax.sharding import PartitionSpec as P


HEADS = 6
GROUP_AXES = ("branch", "pts")

NN = (((1,), (0,)), ((), ()))
NT = (((1,), (1,)), ((), ()))
TN = (((0,), (0,)), ((), ()))


def mm(a, b, dims):
    return lax.dot_general(a, b, dims, preferred_element_type=jnp.float32)


def centered(rows):
    values = rows.astype(jnp.float32)
    center = values - jnp.mean(values, axis=-1, keepdims=True)
    variance = jnp.mean(center * center, axis=-1, keepdims=True)
    return center, lax.rsqrt(variance + 1e-05)


def norm_pullback(center, scale, gain, grad):
    through = grad * gain
    inner = jnp.mean(through * center, axis=-1, keepdims=True)
    grad_center = scale * through - center * (scale * scale * scale * inner)
    return grad_center - jnp.mean(grad_center, axis=-1, keepdims=True)


def as_row(gain):
    return gain[...].reshape(1, -1)


def live_rows(count, rows):
    return (lax.broadcasted_iota(jnp.int32, (rows, 1), 0) < count).astype(jnp.float32)


def masked_pair(pair, head):
    first = lax.broadcasted_iota(jnp.int32, (1, 2 * head), 1) < head
    zero = jnp.zeros((), pair.dtype)
    return jnp.concatenate([jnp.where(first, pair, zero), jnp.where(first, zero, pair)], 0)


def put_pairs(out, rows, head):
    height = 2 * rows.shape[0]
    for k in range(rows.shape[1] // (2 * head)):
        out[k * height : (k + 1) * height, :] = masked_pair(rows[:, 2 * head * k : 2 * head * (k + 1)], head)


def query_side(queries, cot, gain, w_query, w_out, *refs):
    total = (len(refs) - 6) // 2
    sources, outs, count, sems = refs[: total + 1], refs[total + 1 : -2], refs[-2], refs[-1]
    (heads_out, grad_out, live_out), kept = outs[:3], outs[3:]
    copies = [pltpu.make_async_copy(a, b, sems.at[k]) for k, (a, b) in enumerate(zip(sources, kept + (count,)))]
    for copy in copies:
        copy.start()
    center, scale = centered(queries[...])
    query_normed = (center * scale * as_row(gain)).astype(jnp.bfloat16)
    width = queries.shape[1]
    heads = mm(query_normed, w_query[...], NN).astype(jnp.bfloat16)
    put_pairs(heads_out, heads * (1.0 / (width // HEADS) ** 0.5), width // HEADS)
    copies[total].wait()
    live = live_rows(count[0, 0], queries.shape[0])
    live_out[...] = live
    grad_rows = (cot[...].astype(jnp.float32) * live).astype(jnp.bfloat16)
    put_pairs(grad_out, mm(grad_rows, w_out[...], NT).astype(jnp.bfloat16), width // HEADS)
    for copy in copies[:total]:
        copy.wait()


def stage(*refs):
    total = len(refs) // 2
    copies = [pltpu.make_async_copy(refs[k], refs[total + k], refs[-1].at[k]) for k in range(total)]
    for copy in copies:
        copy.start()
    for copy in copies:
        copy.wait()


def join(own, partner, out):
    out[: own.shape[0], :] = own[...]
    out[own.shape[0] :, :] = partner[...]


def where_am_i():
    branch = lax.axis_index("branch")
    return branch % 2, (branch >= lax.axis_size("branch") // 2).astype(jnp.int32)


def ordered(first, second):
    core, _ = where_am_i()
    return jnp.where(core == 0, first, second), jnp.where(core == 0, second, first)


def attend(near, anchors, kind, heads, grads, gain, w_key, w_value, mixed_out, dq_out):
    center, scale = centered(anchors)
    normed = (center * scale * as_row(gain)).astype(jnp.bfloat16)
    keys = mm(normed, w_key[...], NN).astype(jnp.bfloat16)
    values = mm(normed, w_value[...], NN).astype(jnp.bfloat16)
    width = keys.shape[1]
    head = width // HEADS
    rows = kind.shape[1]
    score_scale = 1.0 / head**0.5
    _, volume = where_am_i()
    mine = (kind[...] == 1).astype(jnp.int32) == (volume if near else 1 - volume)
    mine = jnp.concatenate([mine.astype(jnp.int32)] * 2, 1) == 1

    def by_head(x):
        return jnp.concatenate([x[:, :rows], x[:, rows:]], 0)

    key_grads, value_grads = [], []

    def span(k):
        return slice(2 * head * k, 2 * head * (k + 1))

    def lines(k):
        return slice(2 * rows * k, 2 * rows * (k + 1))

    def products(k):
        return mm(keys[:, span(k)], heads[lines(k), :], NT), mm(values[:, span(k)], grads[lines(k), :], NT)

    def soften(scores, grad_probs):
        expo = jnp.exp(scores - jnp.max(scores, axis=0, keepdims=True))
        total = jnp.sum(expo, axis=0, keepdims=True)
        probs = expo * jnp.where(mine, 1.0 / total, 0.0)
        delta = jnp.sum(grad_probs * probs, axis=0, keepdims=True)
        return probs.astype(jnp.bfloat16), (probs * (grad_probs - delta)).astype(jnp.bfloat16)

    def outputs(k, probs, grad_scores):
        key_grads.append(mm(grad_scores, heads[lines(k), :], NN).astype(jnp.bfloat16))
        value_grads.append(mm(probs, grads[lines(k), :], NN).astype(jnp.bfloat16))
        mixed = mm(by_head(probs), masked_pair(values[:, span(k)], head), TN)
        mixed_out[:, span(k)] = mixed.astype(jnp.bfloat16)
        dq = mm(by_head(grad_scores), masked_pair(keys[:, span(k)], head), TN)
        dq_out[:, span(k)] = (dq * score_scale).astype(jnp.bfloat16)

    pairs = width // (2 * head)
    raw = [products(k) for k in range(pairs)]
    soft = [soften(*x) for x in raw]
    for k in range(pairs):
        outputs(k, *soft[k])
    key_grad, value_grad = jnp.concatenate(key_grads, 1), jnp.concatenate(value_grads, 1)
    return mm(key_grad, w_key[...], NT) + mm(value_grad, w_value[...], NT)


def near_side(counts, kind, heads, grads, gain, w_key, w_value, own, partner, *refs):
    both, split, _ = counts
    (got, other), (own_out, send_out, keep_out, mixed_out, dq_out) = refs[:2], refs[2:]
    size = own.shape[0]
    pair = 2 * size
    blocks = [own[...], partner[...], got[: both * pair, :], other[: both * pair, :]]
    for k in range(both, both + split):
        at = slice(k * pair, (k + 1) * pair)
        blocks.append(ordered(got[at, :], other[at, :])[0])
    grad = attend(True, jnp.concatenate(blocks, 0), kind, heads, grads, gain, w_key, w_value, mixed_out, dq_out)
    middle = pair + both * pair
    own_out[...] = grad[:size]
    send_out[:size, :] = grad[size:pair].astype(jnp.bfloat16)
    send_out[size:, :] = grad[middle : middle + both * pair].astype(jnp.bfloat16)
    keep_out[: both * pair, :] = grad[pair:middle]
    keep_out[both * pair :, :] = grad[middle + both * pair :]


def far_side(counts, kind, heads, grads, gain, w_key, w_value, got, other, got_far, other_far, kept, *refs):
    both, split, far = counts
    send_out, keep_out, mixed_out, dq_out = refs
    pair = got.shape[0] // (both + split)
    size = pair // 2
    span = far * pair + size
    blocks = [got_far[...], other_far[...]]
    for k in range(both, both + split):
        at = slice(k * pair, (k + 1) * pair)
        blocks.append(ordered(got[at, :], other[at, :])[1])
    grad = attend(False, jnp.concatenate(blocks, 0), kind, heads, grads, gain, w_key, w_value, mixed_out, dq_out)
    keep_out[:span, :] = grad[:span]
    send_out[:span, :] = grad[span : 2 * span].astype(jnp.bfloat16)
    here, there = ordered(kept[both * pair :, :], grad[2 * span :])
    keep_out[span:, :] = here
    send_out[span:, :] = there.astype(jnp.bfloat16)


def field_rows(live, queries, near, far, w_out, fields):
    residual = queries[...].astype(jnp.float32) + mm(near[...] + far[...], w_out[...], NN)
    fields[...] = (live[...] * residual).astype(jnp.bfloat16)


def query_back(live, queries, cot, near, far, gain, w_query, query_grad):
    center, scale = centered(queries[...])
    back = norm_pullback(center, scale, as_row(gain), mm(near[...] + far[...], w_query[...], NT))
    query_grad[...] = live[...] * (cot[...].astype(jnp.float32) + back)


def add_near(own, keep, got, own_out, *sums):
    size = own.shape[0]
    pair = 2 * size
    own_out[...] = own[...] + got[:size, :].astype(jnp.float32)
    for k, out in enumerate(sums):
        at = k * pair
        out[...] = (keep[at : at + pair, :] + got[size + at : size + at + pair, :].astype(jnp.float32)).astype(out.dtype)


def add_far(keep, got, *sums):
    at = 0
    for out in sums:
        span = slice(at, at + out.shape[0])
        out[...] = (keep[span, :] + got[span, :].astype(jnp.float32)).astype(out.dtype)
        at += out.shape[0]


def add_chips(*refs):
    got, (own, own_out, send_out) = refs[:-3], refs[-3:]
    size = own.shape[0]
    total = got[0][...].astype(jnp.float32)
    for other in got[1:]:
        total = total + other[...].astype(jnp.float32)
    own_out[...] = own[...] + total[:size]
    send_out[...] = total[size:].astype(send_out.dtype)


def anchor_back(anchors, own, got, across, gain, out):
    center, scale = centered(anchors[...])
    grad = own[...] + got[...].astype(jnp.float32) + across[...].astype(jnp.float32)
    out[...] = norm_pullback(center, scale, as_row(gain), grad)


def call(body, outs, *args, staged=(), scratch=()):
    specs = [pl.BlockSpec(memory_space=pltpu.VMEM)] * len(args)
    placed = [pltpu.with_memory_space_constraint(x, pltpu.VMEM) for x in args]
    held = [x if x.size == 1 else pltpu.with_memory_space_constraint(x, pltpu.HBM) for x in staged]
    return pl.pallas_call(
        body,
        out_shape=[pltpu.VMEM(*out) if on_chip else jax.ShapeDtypeStruct(*out) for on_chip, *out in outs],
        in_specs=specs + [pl.BlockSpec(memory_space=pl.ANY if x.size == 1 else pltpu.HBM) for x in staged],
        out_specs=[pl.BlockSpec(memory_space=pltpu.VMEM)] * len(outs),
        scratch_shapes=list(scratch),
        compiler_params=pltpu.CompilerParams(vmem_limit_bytes=32 * 2**20),
    )(*placed, *held)


def exchange_plan(branches, pts):
    top = branches * pts // 2
    nears = [d for d in range(1, top) if not d & pts]
    fars = [d | top for d in nears]
    both = list(zip(nears[:-1:2], nears[1:-1:2]))
    far = list(zip(fars[:-1:2], fars[1:-1:2]))
    return both + [(nears[-1], fars[-1])] + far, (len(both), 1, len(far))


def on_device(sizes, anchors, queries, query_kind, live_count, anchor_gain, query_gain, w_query, w_key, w_value, w_out, cotangent):
    branches, pts = sizes
    group = branches * pts
    plan, counts = exchange_plan(branches, pts)
    both, split, far = counts
    early = both + split

    def send(x, deltas):
        return lax.ppermute(x, GROUP_AXES, [(i, i ^ deltas[(i // pts) % 2]) for i in range(group)])

    def swap(x):
        return send(x, (pts, pts))

    def cross(x):
        return send(x, (group // 2, group // 2))

    size, width = anchors.shape
    rows = queries.shape[0]
    pair = 2 * size
    f32, bf16 = jnp.float32, jnp.bfloat16
    stacked = (HEADS * rows, 2 * width // HEADS)
    partner = swap(anchors)
    needed = (anchors, queries, cotangent, query_gain, w_query, w_out)
    local, queries, cotangent, query_gain, w_query, w_out = call(
        stage,
        [(True, x.shape, x.dtype) for x in needed],
        staged=needed,
        scratch=[pltpu.SemaphoreType.DMA((len(needed),))],
    )
    (chip,) = call(join, [(True, (pair, width), bf16)], local, partner)
    got = []
    for step in plan:
        got.append(send(chip, step))
    across = cross(anchors)
    inputs = (anchor_gain, w_key, w_value, query_kind.reshape(1, -1))
    heads, grads, live, anchor_gain, w_key, w_value, query_kind = call(
        query_side,
        [(True, stacked, bf16)] * 2 + [(True, (rows, 1), f32)] + [(True, x.shape, x.dtype) for x in inputs],
        queries,
        cotangent,
        query_gain,
        w_query,
        w_out,
        staged=inputs + (live_count.reshape(1, 1),),
        scratch=[pltpu.SMEM((1, 1), jnp.int32), pltpu.SemaphoreType.DMA((len(inputs) + 1,))],
    )
    got_near = jnp.concatenate(got[:early], 0)
    other_near = swap(got_near)
    got_far = jnp.concatenate([across] + got[early:], 0)
    other_far = swap(got_far)
    common = (query_kind, heads, grads, anchor_gain, w_key, w_value)
    rowwise = [(True, (rows, width), bf16)] * 2
    own, send_near, keep_near, mixed_near, dq_near = call(
        functools.partial(near_side, counts),
        [(True, (size, width), f32), (True, (size + pair * both, width), bf16), (True, (pair * early, width), f32)] + rowwise,
        *common,
        local,
        partner,
        got_near,
        other_near,
    )
    back_near = swap(send_near)
    send_far, keep_far, mixed_far, dq_far = call(
        functools.partial(far_side, counts),
        [(True, (size + pair * (far + split), width), bf16), (True, (size + pair * (far + split), width), f32)] + rowwise,
        *common,
        got_near,
        other_near,
        got_far,
        other_far,
        keep_near,
    )
    back_far = swap(send_far)
    own, *sums = call(
        add_near, [(True, (size, width), f32)] + [(True, (pair, width), bf16)] * both, own, keep_near, back_near
    )
    across, *more = call(
        add_far, [(True, (size, width), bf16)] + [(True, (pair, width), bf16)] * (far + split), keep_far, back_far
    )
    sums += more[far:] + more[:far]
    arrived = []
    for part, step in zip(sums, plan):
        arrived.append(send(part, step))
    across = cross(across)
    (fields,) = call(field_rows, [(False, (rows, width), bf16)], live, queries, mixed_near, mixed_far, w_out)
    (query_grad,) = call(
        query_back, [(False, (rows, width), f32)],
        live, queries, cotangent, dq_near, dq_far, query_gain, w_query,
    )
    own, last = call(add_chips, [(True, (size, width), f32), (True, (size, width), bf16)], *arrived, own)
    last = swap(last)
    (anchor_grad,) = call(anchor_back, [(False, (size, width), f32)], local, own, last, across, anchor_gain)
    return fields, query_grad, anchor_grad


def solution(mesh):
    split = P(("car",) + GROUP_AXES, None)
    flat = P(("car",) + GROUP_AXES)
    sizes = mesh.shape["branch"], mesh.shape["pts"]

    def body(*args):
        return on_device(sizes, *args)

    return jax.shard_map(
        body,
        mesh=mesh,
        in_specs=(split, split, flat, flat, P(), P(), P(), P(), P(), P(), split),
        out_specs=(split, split, split),
        check_vma=False,
    )
```

```python
import functools

import jax
import jax.numpy as jnp
from jax import lax
from jax.experimental import pallas as pl
from jax.experimental.pallas import tpu as pltpu
from jax.sharding import PartitionSpec as P


HEADS = 6
GROUP_AXES = ("branch", "pts")

NN = (((1,), (0,)), ((), ()))
NT = (((1,), (1,)), ((), ()))
TN = (((0,), (0,)), ((), ()))


def mm(a, b, dims):
    return lax.dot_general(a, b, dims, preferred_element_type=jnp.float32)


def centered(rows):
    values = rows.astype(jnp.float32)
    center = values - jnp.mean(values, axis=-1, keepdims=True)
    variance = jnp.mean(center * center, axis=-1, keepdims=True)
    return center, lax.rsqrt(variance + 1e-05)


def norm_pullback(center, scale, gain, grad):
    through = grad * gain
    inner = jnp.mean(through * center, axis=-1, keepdims=True)
    grad_center = scale * through - center * (scale * scale * scale * inner)
    return grad_center - jnp.mean(grad_center, axis=-1, keepdims=True)


def as_row(gain):
    return gain[...].reshape(1, -1)


def live_rows(count, rows):
    return (lax.broadcasted_iota(jnp.int32, (rows, 1), 0) < count).astype(jnp.float32)


def masked_pair(pair, head):
    first = lax.broadcasted_iota(jnp.int32, (1, 2 * head), 1) < head
    zero = jnp.zeros((), pair.dtype)
    return jnp.concatenate([jnp.where(first, pair, zero), jnp.where(first, zero, pair)], 0)


def put_pairs(out, rows, head):
    height = 2 * rows.shape[0]
    for k in range(rows.shape[1] // (2 * head)):
        out[k * height : (k + 1) * height, :] = masked_pair(rows[:, 2 * head * k : 2 * head * (k + 1)], head)


def query_side(queries, cot, gain, w_query, w_out, *refs):
    total = (len(refs) - 6) // 2
    sources, outs, count, sems = refs[: total + 1], refs[total + 1 : -2], refs[-2], refs[-1]
    (heads_out, grad_out, live_out), kept = outs[:3], outs[3:]
    copies = [pltpu.make_async_copy(a, b, sems.at[k]) for k, (a, b) in enumerate(zip(sources, kept + (count,)))]
    for copy in copies:
        copy.start()
    center, scale = centered(queries[...])
    query_normed = (center * scale * as_row(gain)).astype(jnp.bfloat16)
    width = queries.shape[1]
    heads = mm(query_normed, w_query[...], NN).astype(jnp.bfloat16)
    put_pairs(heads_out, heads * (1.0 / (width // HEADS) ** 0.5), width // HEADS)
    copies[total].wait()
    live = live_rows(count[0, 0], queries.shape[0])
    live_out[...] = live
    grad_rows = (cot[...].astype(jnp.float32) * live).astype(jnp.bfloat16)
    put_pairs(grad_out, mm(grad_rows, w_out[...], NT).astype(jnp.bfloat16), width // HEADS)
    for copy in copies[:total]:
        copy.wait()


def stage(*refs):
    total = len(refs) // 2
    copies = [pltpu.make_async_copy(refs[k], refs[total + k], refs[-1].at[k]) for k in range(total)]
    for copy in copies:
        copy.start()
    for copy in copies:
        copy.wait()


def pack(*refs):
    at = 0
    for ref in refs[:-1]:
        refs[-1][at : at + ref.shape[0], :] = ref[...]
        at += ref.shape[0]


def join(own, partner, out):
    out[: own.shape[0], :] = own[...]
    out[own.shape[0] :, :] = partner[...]


def where_am_i():
    branch = lax.axis_index("branch")
    return branch % 2, (branch >= lax.axis_size("branch") // 2).astype(jnp.int32)


def ordered(first, second):
    core, _ = where_am_i()
    return jnp.where(core == 0, first, second), jnp.where(core == 0, second, first)


def attend(near, anchors, kind, heads, grads, gain, w_key, w_value, mixed_out, dq_out):
    center, scale = centered(anchors)
    normed = (center * scale * as_row(gain)).astype(jnp.bfloat16)
    keys = mm(normed, w_key[...], NN).astype(jnp.bfloat16)
    values = mm(normed, w_value[...], NN).astype(jnp.bfloat16)
    width = keys.shape[1]
    head = width // HEADS
    rows = kind.shape[1]
    score_scale = 1.0 / head**0.5
    _, volume = where_am_i()
    mine = (kind[...] == 1).astype(jnp.int32) == (volume if near else 1 - volume)
    mine = jnp.concatenate([mine.astype(jnp.int32)] * 2, 1) == 1

    def by_head(x):
        return jnp.concatenate([x[:, :rows], x[:, rows:]], 0)

    key_grads, value_grads = [], []

    def span(k):
        return slice(2 * head * k, 2 * head * (k + 1))

    def lines(k):
        return slice(2 * rows * k, 2 * rows * (k + 1))

    def products(k):
        return mm(keys[:, span(k)], heads[lines(k), :], NT), mm(values[:, span(k)], grads[lines(k), :], NT)

    def soften(scores, grad_probs):
        expo = jnp.exp(scores - jnp.max(scores, axis=0, keepdims=True))
        total = jnp.sum(expo, axis=0, keepdims=True)
        probs = expo * jnp.where(mine, 1.0 / total, 0.0)
        delta = jnp.sum(grad_probs * probs, axis=0, keepdims=True)
        return probs.astype(jnp.bfloat16), (probs * (grad_probs - delta)).astype(jnp.bfloat16)

    def outputs(k, probs, grad_scores):
        key_grads.append(mm(grad_scores, heads[lines(k), :], NN).astype(jnp.bfloat16))
        value_grads.append(mm(probs, grads[lines(k), :], NN).astype(jnp.bfloat16))
        mixed = mm(by_head(probs), masked_pair(values[:, span(k)], head), TN)
        mixed_out[:, span(k)] = mixed.astype(jnp.bfloat16)
        dq = mm(by_head(grad_scores), masked_pair(keys[:, span(k)], head), TN)
        dq_out[:, span(k)] = (dq * score_scale).astype(jnp.bfloat16)

    pairs = width // (2 * head)
    raw = [products(k) for k in range(pairs)]
    soft = [soften(*x) for x in raw]
    for k in range(pairs):
        outputs(k, *soft[k])
    key_grad, value_grad = jnp.concatenate(key_grads, 1), jnp.concatenate(value_grads, 1)
    return mm(key_grad, w_key[...], NT) + mm(value_grad, w_value[...], NT)


def near_side(counts, kind, heads, grads, gain, w_key, w_value, own, partner, *refs):
    both, split, _ = counts
    (got, other), (own_out, send_out, keep_out, mixed_out, dq_out) = refs[:2], refs[2:]
    size = own.shape[0]
    pair = 2 * size
    blocks = [own[...], partner[...], got[: both * pair, :], other[: both * pair, :]]
    for k in range(both, both + split):
        at = slice(k * pair, (k + 1) * pair)
        blocks.append(ordered(got[at, :], other[at, :])[0])
    grad = attend(True, jnp.concatenate(blocks, 0), kind, heads, grads, gain, w_key, w_value, mixed_out, dq_out)
    middle = pair + both * pair
    own_out[...] = grad[:size]
    send_out[:size, :] = grad[size:pair].astype(jnp.bfloat16)
    send_out[size:, :] = grad[middle : middle + both * pair].astype(jnp.bfloat16)
    keep_out[: both * pair, :] = grad[pair:middle]
    keep_out[both * pair :, :] = grad[middle + both * pair :]


def far_side(counts, kind, heads, grads, gain, w_key, w_value, got, other, got_far, other_far, kept, *refs):
    both, split, far = counts
    send_out, keep_out, mixed_out, dq_out = refs
    pair = got.shape[0] // (both + split)
    size = pair // 2
    span = far * pair + size
    blocks = [got_far[...], other_far[...]]
    for k in range(both, both + split):
        at = slice(k * pair, (k + 1) * pair)
        blocks.append(ordered(got[at, :], other[at, :])[1])
    grad = attend(False, jnp.concatenate(blocks, 0), kind, heads, grads, gain, w_key, w_value, mixed_out, dq_out)
    keep_out[:span, :] = grad[:span]
    send_out[:span, :] = grad[span : 2 * span].astype(jnp.bfloat16)
    here, there = ordered(kept[both * pair :, :], grad[2 * span :])
    keep_out[span:, :] = here
    send_out[span:, :] = there.astype(jnp.bfloat16)


def field_rows(live, queries, near, far, w_out, fields):
    residual = queries[...].astype(jnp.float32) + mm(near[...] + far[...], w_out[...], NN)
    fields[...] = (live[...] * residual).astype(jnp.bfloat16)


def query_back(live, queries, cot, near, far, gain, w_query, query_grad):
    center, scale = centered(queries[...])
    back = norm_pullback(center, scale, as_row(gain), mm(near[...] + far[...], w_query[...], NT))
    query_grad[...] = live[...] * (cot[...].astype(jnp.float32) + back)


def add_near(own, keep, got, own_out, *sums):
    size = own.shape[0]
    pair = 2 * size
    own_out[...] = own[...] + got[:size, :].astype(jnp.float32)
    for k, out in enumerate(sums):
        at = k * pair
        out[...] = (keep[at : at + pair, :] + got[size + at : size + at + pair, :].astype(jnp.float32)).astype(out.dtype)


def add_far(keep, got, *sums):
    at = 0
    for out in sums:
        span = slice(at, at + out.shape[0])
        out[...] = (keep[span, :] + got[span, :].astype(jnp.float32)).astype(out.dtype)
        at += out.shape[0]


def add_chips(*refs):
    got, (own, own_out, send_out) = refs[:-3], refs[-3:]
    size = own.shape[0]
    total = got[0][...].astype(jnp.float32)
    for other in got[1:]:
        total = total + other[...].astype(jnp.float32)
    own_out[...] = own[...] + total[:size]
    send_out[...] = total[size:].astype(send_out.dtype)


def anchor_back(anchors, own, got, across, gain, out):
    center, scale = centered(anchors[...])
    grad = own[...] + got[...].astype(jnp.float32) + across[...].astype(jnp.float32)
    out[...] = norm_pullback(center, scale, as_row(gain), grad)


def call(body, outs, *args, staged=(), scratch=()):
    specs = [pl.BlockSpec(memory_space=pltpu.VMEM)] * len(args)
    placed = [pltpu.with_memory_space_constraint(x, pltpu.VMEM) for x in args]
    held = [x if x.size == 1 else pltpu.with_memory_space_constraint(x, pltpu.HBM) for x in staged]
    return pl.pallas_call(
        body,
        out_shape=[pltpu.VMEM(*out) if on_chip else jax.ShapeDtypeStruct(*out) for on_chip, *out in outs],
        in_specs=specs + [pl.BlockSpec(memory_space=pl.ANY if x.size == 1 else pltpu.HBM) for x in staged],
        out_specs=[pl.BlockSpec(memory_space=pltpu.VMEM)] * len(outs),
        scratch_shapes=list(scratch),
        compiler_params=pltpu.CompilerParams(vmem_limit_bytes=32 * 2**20),
    )(*placed, *held)


def exchange_plan(branches, pts):
    top = branches * pts // 2
    nears = [d for d in range(1, top) if not d & pts]
    fars = [d | top for d in nears]
    both = list(zip(nears[:-1:2], nears[1:-1:2]))
    far = list(zip(fars[:-1:2], fars[1:-1:2]))
    return both + [(nears[-1], fars[-1])] + far, (len(both), 1, len(far))


def on_device(sizes, anchors, queries, query_kind, live_count, anchor_gain, query_gain, w_query, w_key, w_value, w_out, cotangent):
    branches, pts = sizes
    group = branches * pts
    plan, counts = exchange_plan(branches, pts)
    both, split, far = counts
    early = both + split

    def send(x, deltas):
        return lax.ppermute(x, GROUP_AXES, [(i, i ^ deltas[(i // pts) % 2]) for i in range(group)])

    def swap(x):
        return send(x, (pts, pts))

    def cross(x):
        return send(x, (group // 2, group // 2))

    size, width = anchors.shape
    rows = queries.shape[0]
    pair = 2 * size
    f32, bf16 = jnp.float32, jnp.bfloat16
    stacked = (HEADS * rows, 2 * width // HEADS)
    partner = swap(anchors)
    needed = (anchors, queries, cotangent, query_gain, w_query, w_out)
    local, queries, cotangent, query_gain, w_query, w_out = call(
        stage,
        [(True, x.shape, x.dtype) for x in needed],
        staged=needed,
        scratch=[pltpu.SemaphoreType.DMA((len(needed),))],
    )
    (chip,) = call(join, [(True, (pair, width), bf16)], local, partner)
    got = []
    for step in plan:
        got.append(send(chip, step))
    across = cross(anchors)
    inputs = (anchor_gain, w_key, w_value, query_kind.reshape(1, -1))
    heads, grads, live, anchor_gain, w_key, w_value, query_kind = call(
        query_side,
        [(True, stacked, bf16)] * 2 + [(True, (rows, 1), f32)] + [(True, x.shape, x.dtype) for x in inputs],
        queries,
        cotangent,
        query_gain,
        w_query,
        w_out,
        staged=inputs + (live_count.reshape(1, 1),),
        scratch=[pltpu.SMEM((1, 1), jnp.int32), pltpu.SemaphoreType.DMA((len(inputs) + 1,))],
    )
    (got_near,) = call(pack, [(True, (pair * early, width), bf16)], *got[:early])
    other_near = swap(got_near)
    got_far = jnp.concatenate([across] + got[early:], 0)
    other_far = swap(got_far)
    common = (query_kind, heads, grads, anchor_gain, w_key, w_value)
    rowwise = [(True, (rows, width), bf16)] * 2
    own, send_near, keep_near, mixed_near, dq_near = call(
        functools.partial(near_side, counts),
        [(True, (size, width), f32), (True, (size + pair * both, width), bf16), (True, (pair * early, width), f32)] + rowwise,
        *common,
        local,
        partner,
        got_near,
        other_near,
    )
    back_near = swap(send_near)
    send_far, keep_far, mixed_far, dq_far = call(
        functools.partial(far_side, counts),
        [(True, (size + pair * (far + split), width), bf16), (True, (size + pair * (far + split), width), f32)] + rowwise,
        *common,
        got_near,
        other_near,
        got_far,
        other_far,
        keep_near,
    )
    back_far = swap(send_far)
    own, *sums = call(
        add_near, [(True, (size, width), f32)] + [(True, (pair, width), bf16)] * both, own, keep_near, back_near
    )
    across, *more = call(
        add_far, [(True, (size, width), bf16)] + [(True, (pair, width), bf16)] * (far + split), keep_far, back_far
    )
    sums += more[far:] + more[:far]
    arrived = []
    for part, step in zip(sums, plan):
        arrived.append(send(part, step))
    across = cross(across)
    (fields,) = call(field_rows, [(False, (rows, width), bf16)], live, queries, mixed_near, mixed_far, w_out)
    (query_grad,) = call(
        query_back, [(False, (rows, width), f32)],
        live, queries, cotangent, dq_near, dq_far, query_gain, w_query,
    )
    own, last = call(add_chips, [(True, (size, width), f32), (True, (size, width), bf16)], *arrived, own)
    last = swap(last)
    (anchor_grad,) = call(anchor_back, [(False, (size, width), f32)], local, own, last, across, anchor_gain)
    return fields, query_grad, anchor_grad


def solution(mesh):
    split = P(("car",) + GROUP_AXES, None)
    flat = P(("car",) + GROUP_AXES)
    sizes = mesh.shape["branch"], mesh.shape["pts"]

    def body(*args):
        return on_device(sizes, *args)

    return jax.shard_map(
        body,
        mesh=mesh,
        in_specs=(split, split, flat, flat, P(), P(), P(), P(), P(), P(), split),
        out_specs=(split, split, split),
        check_vma=False,
    )
```

```python
import functools

import jax
import jax.numpy as jnp
from jax import lax
from jax.experimental import pallas as pl
from jax.experimental.pallas import tpu as pltpu
from jax.sharding import PartitionSpec as P


HEADS = 6
GROUP_AXES = ("branch", "pts")

NN = (((1,), (0,)), ((), ()))
NT = (((1,), (1,)), ((), ()))
TN = (((0,), (0,)), ((), ()))


def mm(a, b, dims):
    return lax.dot_general(a, b, dims, preferred_element_type=jnp.float32)


def centered(rows):
    values = rows.astype(jnp.float32)
    center = values - jnp.mean(values, axis=-1, keepdims=True)
    variance = jnp.mean(center * center, axis=-1, keepdims=True)
    return center, lax.rsqrt(variance + 1e-05)


def norm_pullback(center, scale, gain, grad):
    through = grad * gain
    inner = jnp.mean(through * center, axis=-1, keepdims=True)
    grad_center = scale * through - center * (scale * scale * scale * inner)
    return grad_center - jnp.mean(grad_center, axis=-1, keepdims=True)


def as_row(gain):
    return gain[...].reshape(1, -1)


def live_rows(count, rows):
    return (lax.broadcasted_iota(jnp.int32, (rows, 1), 0) < count).astype(jnp.float32)


def masked_pair(pair, head):
    first = lax.broadcasted_iota(jnp.int32, (1, 2 * head), 1) < head
    zero = jnp.zeros((), pair.dtype)
    return jnp.concatenate([jnp.where(first, pair, zero), jnp.where(first, zero, pair)], 0)


def put_pairs(out, rows, head):
    height = 2 * rows.shape[0]
    for k in range(rows.shape[1] // (2 * head)):
        out[k * height : (k + 1) * height, :] = masked_pair(rows[:, 2 * head * k : 2 * head * (k + 1)], head)


def query_side(queries, cot, gain, w_query, w_out, *refs):
    total = (len(refs) - 6) // 2
    sources, outs, count, sems = refs[: total + 1], refs[total + 1 : -2], refs[-2], refs[-1]
    (heads_out, grad_out, live_out), kept = outs[:3], outs[3:]
    copies = [pltpu.make_async_copy(a, b, sems.at[k]) for k, (a, b) in enumerate(zip(sources, kept + (count,)))]
    for copy in copies:
        copy.start()
    center, scale = centered(queries[...])
    query_normed = (center * scale * as_row(gain)).astype(jnp.bfloat16)
    width = queries.shape[1]
    heads = mm(query_normed, w_query[...], NN).astype(jnp.bfloat16)
    put_pairs(heads_out, heads * (1.0 / (width // HEADS) ** 0.5), width // HEADS)
    copies[total].wait()
    live = live_rows(count[0, 0], queries.shape[0])
    live_out[...] = live
    grad_rows = (cot[...].astype(jnp.float32) * live).astype(jnp.bfloat16)
    put_pairs(grad_out, mm(grad_rows, w_out[...], NT).astype(jnp.bfloat16), width // HEADS)
    for copy in copies[:total]:
        copy.wait()


def stage(*refs):
    total = len(refs) // 2
    copies = [pltpu.make_async_copy(refs[k], refs[total + k], refs[-1].at[k]) for k in range(total)]
    for copy in copies:
        copy.start()
    for copy in copies:
        copy.wait()


def pack(*refs):
    at = 0
    for ref in refs[:-1]:
        refs[-1][at : at + ref.shape[0], :] = ref[...]
        at += ref.shape[0]


def join(own, partner, gain, out, mine):
    size = own.shape[0]
    center, scale = centered(jnp.concatenate([own[...], partner[...]], 0))
    normed = (center * scale * as_row(gain)).astype(jnp.bfloat16)
    out[...] = normed
    mine[...] = normed[:size]


def fold(heads, grads, w_key, w_value, heads_back, grads_back):
    lanes = heads.shape[1]
    height = heads.shape[0] * lanes // w_key.shape[1]
    for rows, weight, out in ((heads, w_key, heads_back), (grads, w_value, grads_back)):
        for k in range(w_key.shape[1] // lanes):
            lines = slice(k * height, (k + 1) * height)
            product = mm(rows[lines, :], weight[:, k * lanes : (k + 1) * lanes], NT)
            out[lines, :] = product.astype(out.dtype)


def where_am_i():
    branch = lax.axis_index("branch")
    return branch % 2, (branch >= lax.axis_size("branch") // 2).astype(jnp.int32)


def ordered(first, second):
    core, _ = where_am_i()
    return jnp.where(core == 0, first, second), jnp.where(core == 0, second, first)


def attend(near, normed, kind, heads, grads, heads_back, grads_back, w_key, w_value, mixed_out, dq_out):
    keys = mm(normed, w_key[...], NN).astype(jnp.bfloat16)
    values = mm(normed, w_value[...], NN).astype(jnp.bfloat16)
    width = keys.shape[1]
    head = width // HEADS
    rows = kind.shape[1]
    score_scale = 1.0 / head**0.5
    _, volume = where_am_i()
    mine = (kind[...] == 1).astype(jnp.int32) == (volume if near else 1 - volume)
    mine = jnp.concatenate([mine.astype(jnp.int32)] * 2, 1) == 1

    def by_head(x):
        return jnp.concatenate([x[:, :rows], x[:, rows:]], 0)

    def span(k):
        return slice(2 * head * k, 2 * head * (k + 1))

    def lines(k):
        return slice(2 * rows * k, 2 * rows * (k + 1))

    def products(k):
        return mm(keys[:, span(k)], heads[lines(k), :], NT), mm(values[:, span(k)], grads[lines(k), :], NT)

    def soften(scores, grad_probs):
        expo = jnp.exp(scores - jnp.max(scores, axis=0, keepdims=True))
        total = jnp.sum(expo, axis=0, keepdims=True)
        probs = expo * jnp.where(mine, 1.0 / total, 0.0)
        delta = jnp.sum(grad_probs * probs, axis=0, keepdims=True)
        return probs.astype(jnp.bfloat16), (probs * (grad_probs - delta)).astype(jnp.bfloat16)

    pairs = range(width // (2 * head))
    raw = [products(k) for k in pairs]
    soft = [soften(*x) for x in raw]
    result = mm(jnp.concatenate([x[1] for x in soft], 1), heads_back[...], NN)
    result = result + mm(jnp.concatenate([x[0] for x in soft], 1), grads_back[...], NN)
    for k in pairs:
        mixed = mm(by_head(soft[k][0]), masked_pair(values[:, span(k)], head), TN)
        mixed_out[:, span(k)] = mixed.astype(jnp.bfloat16)
        dq = mm(by_head(soft[k][1]), masked_pair(keys[:, span(k)], head), TN)
        dq_out[:, span(k)] = (dq * score_scale).astype(jnp.bfloat16)
    return result


def near_side(counts, kind, heads, grads, heads_back, grads_back, w_key, w_value, chip, *refs):
    both, split, _ = counts
    (got, other), (own_out, send_out, keep_out, mixed_out, dq_out) = refs[:2], refs[2:]
    pair = chip.shape[0]
    size = pair // 2
    blocks = [chip[...], got[: both * pair, :], other[: both * pair, :]]
    for k in range(both, both + split):
        at = slice(k * pair, (k + 1) * pair)
        blocks.append(ordered(got[at, :], other[at, :])[0])
    grad = attend(True, jnp.concatenate(blocks, 0), kind, heads, grads, heads_back, grads_back, w_key, w_value, mixed_out, dq_out)
    middle = pair + both * pair
    own_out[...] = grad[:size]
    send_out[:size, :] = grad[size:pair].astype(jnp.bfloat16)
    send_out[size:, :] = grad[middle : middle + both * pair].astype(jnp.bfloat16)
    keep_out[: both * pair, :] = grad[pair:middle]
    keep_out[both * pair :, :] = grad[middle + both * pair :]


def far_side(counts, kind, heads, grads, heads_back, grads_back, w_key, w_value, got, other, got_far, other_far, kept, *refs):
    both, split, far = counts
    send_out, keep_out, mixed_out, dq_out = refs
    pair = got.shape[0] // (both + split)
    size = pair // 2
    span = far * pair + size
    blocks = [got_far[...], other_far[...]]
    for k in range(both, both + split):
        at = slice(k * pair, (k + 1) * pair)
        blocks.append(ordered(got[at, :], other[at, :])[1])
    grad = attend(False, jnp.concatenate(blocks, 0), kind, heads, grads, heads_back, grads_back, w_key, w_value, mixed_out, dq_out)
    keep_out[:span, :] = grad[:span]
    send_out[:span, :] = grad[span : 2 * span].astype(jnp.bfloat16)
    here, there = ordered(kept[both * pair :, :], grad[2 * span :])
    keep_out[span:, :] = here
    send_out[span:, :] = there.astype(jnp.bfloat16)


def field_rows(live, queries, near, far, w_out, fields):
    residual = queries[...].astype(jnp.float32) + mm(near[...] + far[...], w_out[...], NN)
    fields[...] = (live[...] * residual).astype(jnp.bfloat16)


def query_back(live, queries, cot, near, far, gain, w_query, query_grad):
    center, scale = centered(queries[...])
    back = norm_pullback(center, scale, as_row(gain), mm(near[...] + far[...], w_query[...], NT))
    query_grad[...] = live[...] * (cot[...].astype(jnp.float32) + back)


def add_near(own, keep, got, own_out, *sums):
    size = own.shape[0]
    pair = 2 * size
    own_out[...] = own[...] + got[:size, :].astype(jnp.float32)
    for k, out in enumerate(sums):
        at = k * pair
        out[...] = (keep[at : at + pair, :] + got[size + at : size + at + pair, :].astype(jnp.float32)).astype(out.dtype)


def add_far(keep, got, *sums):
    at = 0
    for out in sums:
        span = slice(at, at + out.shape[0])
        out[...] = (keep[span, :] + got[span, :].astype(jnp.float32)).astype(out.dtype)
        at += out.shape[0]


def add_chips(*refs):
    got, (own, own_out, send_out) = refs[:-3], refs[-3:]
    size = own.shape[0]
    total = got[0][...].astype(jnp.float32)
    for other in got[1:]:
        total = total + other[...].astype(jnp.float32)
    own_out[...] = own[...] + total[:size]
    send_out[...] = total[size:].astype(send_out.dtype)


def anchor_back(anchors, own, got, across, gain, out):
    center, scale = centered(anchors[...])
    grad = own[...] + got[...].astype(jnp.float32) + across[...].astype(jnp.float32)
    out[...] = norm_pullback(center, scale, as_row(gain), grad)


def call(body, outs, *args, staged=(), scratch=()):
    specs = [pl.BlockSpec(memory_space=pltpu.VMEM)] * len(args)
    placed = [pltpu.with_memory_space_constraint(x, pltpu.VMEM) for x in args]
    held = [x if x.size == 1 else pltpu.with_memory_space_constraint(x, pltpu.HBM) for x in staged]
    return pl.pallas_call(
        body,
        out_shape=[pltpu.VMEM(*out) if on_chip else jax.ShapeDtypeStruct(*out) for on_chip, *out in outs],
        in_specs=specs + [pl.BlockSpec(memory_space=pl.ANY if x.size == 1 else pltpu.HBM) for x in staged],
        out_specs=[pl.BlockSpec(memory_space=pltpu.VMEM)] * len(outs),
        scratch_shapes=list(scratch),
        compiler_params=pltpu.CompilerParams(vmem_limit_bytes=32 * 2**20),
    )(*placed, *held)


def exchange_plan(branches, pts):
    top = branches * pts // 2
    nears = [d for d in range(1, top) if not d & pts]
    fars = [d | top for d in nears]
    both = list(zip(nears[:-1:2], nears[1:-1:2]))
    far = list(zip(fars[:-1:2], fars[1:-1:2]))
    return both + [(nears[-1], fars[-1])] + far, (len(both), 1, len(far))


def on_device(sizes, anchors, queries, query_kind, live_count, anchor_gain, query_gain, w_query, w_key, w_value, w_out, cotangent):
    branches, pts = sizes
    group = branches * pts
    plan, counts = exchange_plan(branches, pts)
    both, split, far = counts
    early = both + split

    def send(x, deltas):
        return lax.ppermute(x, GROUP_AXES, [(i, i ^ deltas[(i // pts) % 2]) for i in range(group)])

    def swap(x):
        return send(x, (pts, pts))

    def cross(x):
        return send(x, (group // 2, group // 2))

    size, width = anchors.shape
    rows = queries.shape[0]
    pair = 2 * size
    f32, bf16 = jnp.float32, jnp.bfloat16
    stacked = (HEADS * rows, 2 * width // HEADS)
    partner = swap(anchors)
    needed = (anchors, anchor_gain, queries, cotangent, query_gain, w_query, w_out)
    local, anchor_gain, queries, cotangent, query_gain, w_query, w_out = call(
        stage,
        [(True, x.shape, x.dtype) for x in needed],
        staged=needed,
        scratch=[pltpu.SemaphoreType.DMA((len(needed),))],
    )
    chip, mine = call(join, [(True, (pair, width), bf16), (True, (size, width), bf16)], local, partner, anchor_gain)
    got = []
    for step in plan:
        got.append(send(chip, step))
    across = cross(mine)
    inputs = (w_key, w_value, query_kind.reshape(1, -1))
    heads, grads, live, w_key, w_value, query_kind = call(
        query_side,
        [(True, stacked, bf16)] * 2 + [(True, (rows, 1), f32)] + [(True, x.shape, x.dtype) for x in inputs],
        queries,
        cotangent,
        query_gain,
        w_query,
        w_out,
        staged=inputs + (live_count.reshape(1, 1),),
        scratch=[pltpu.SMEM((1, 1), jnp.int32), pltpu.SemaphoreType.DMA((len(inputs) + 1,))],
    )
    (got_near,) = call(pack, [(True, (pair * early, width), bf16)], *got[:early])
    other_near = swap(got_near)
    got_far = jnp.concatenate([across] + got[early:], 0)
    other_far = swap(got_far)
    folded = [(True, (HEADS * rows, width), bf16)] * 2
    heads_back, grads_back = call(fold, folded, heads, grads, w_key, w_value)
    common = (query_kind, heads, grads, heads_back, grads_back, w_key, w_value)
    rowwise = [(True, (rows, width), bf16)] * 2
    own, send_near, keep_near, mixed_near, dq_near = call(
        functools.partial(near_side, counts),
        [(True, (size, width), f32), (True, (size + pair * both, width), bf16), (True, (pair * early, width), f32)] + rowwise,
        *common,
        chip,
        got_near,
        other_near,
    )
    back_near = swap(send_near)
    send_far, keep_far, mixed_far, dq_far = call(
        functools.partial(far_side, counts),
        [(True, (size + pair * (far + split), width), bf16), (True, (size + pair * (far + split), width), f32)] + rowwise,
        *common,
        got_near,
        other_near,
        got_far,
        other_far,
        keep_near,
    )
    back_far = swap(send_far)
    own, *sums = call(
        add_near, [(True, (size, width), f32)] + [(True, (pair, width), bf16)] * both, own, keep_near, back_near
    )
    across, *more = call(
        add_far, [(True, (size, width), bf16)] + [(True, (pair, width), bf16)] * (far + split), keep_far, back_far
    )
    sums += more[far:] + more[:far]
    arrived = []
    for part, step in zip(sums, plan):
        arrived.append(send(part, step))
    across = cross(across)
    (fields,) = call(field_rows, [(False, (rows, width), bf16)], live, queries, mixed_near, mixed_far, w_out)
    (query_grad,) = call(
        query_back, [(False, (rows, width), f32)],
        live, queries, cotangent, dq_near, dq_far, query_gain, w_query,
    )
    own, last = call(add_chips, [(True, (size, width), f32), (True, (size, width), bf16)], *arrived, own)
    last = swap(last)
    (anchor_grad,) = call(anchor_back, [(True, (size, width), f32)], local, own, last, across, anchor_gain)
    return fields, query_grad, anchor_grad


def solution(mesh):
    split = P(("car",) + GROUP_AXES, None)
    flat = P(("car",) + GROUP_AXES)
    sizes = mesh.shape["branch"], mesh.shape["pts"]

    def body(*args):
        return on_device(sizes, *args)

    return jax.shard_map(
        body,
        mesh=mesh,
        in_specs=(split, split, flat, flat, P(), P(), P(), P(), P(), P(), split),
        out_specs=(split, split, split),
        check_vma=False,
    )
```

```python
import functools

import jax
import jax.numpy as jnp
from jax import lax
from jax.experimental import pallas as pl
from jax.experimental.pallas import tpu as pltpu
from jax.sharding import PartitionSpec as P


HEADS = 6
GROUP_AXES = ("branch", "pts")

NN = (((1,), (0,)), ((), ()))
NT = (((1,), (1,)), ((), ()))
TN = (((0,), (0,)), ((), ()))


def mm(a, b, dims):
    return lax.dot_general(a, b, dims, preferred_element_type=jnp.float32)


def centered(rows):
    values = rows.astype(jnp.float32)
    center = values - jnp.mean(values, axis=-1, keepdims=True)
    variance = jnp.mean(center * center, axis=-1, keepdims=True)
    return center, lax.rsqrt(variance + 1e-05)


def norm_pullback(center, scale, gain, grad):
    through = grad * gain
    inner = jnp.mean(through * center, axis=-1, keepdims=True)
    grad_center = scale * through - center * (scale * scale * scale * inner)
    return grad_center - jnp.mean(grad_center, axis=-1, keepdims=True)


def as_row(gain):
    return gain[...].reshape(1, -1)


def live_rows(count, rows):
    return (lax.broadcasted_iota(jnp.int32, (rows, 1), 0) < count).astype(jnp.float32)


def masked_pair(pair, head):
    first = lax.broadcasted_iota(jnp.int32, (1, 2 * head), 1) < head
    zero = jnp.zeros((), pair.dtype)
    return jnp.concatenate([jnp.where(first, pair, zero), jnp.where(first, zero, pair)], 0)


def put_pairs(out, rows, head):
    height = 2 * rows.shape[0]
    for k in range(rows.shape[1] // (2 * head)):
        out[k * height : (k + 1) * height, :] = masked_pair(rows[:, 2 * head * k : 2 * head * (k + 1)], head)


def query_side(queries, cot, gain, w_query, w_out, *refs):
    total = (len(refs) - 6) // 2
    sources, outs, count, sems = refs[: total + 1], refs[total + 1 : -2], refs[-2], refs[-1]
    (heads_out, grad_out, live_out), kept = outs[:3], outs[3:]
    copies = [pltpu.make_async_copy(a, b, sems.at[k]) for k, (a, b) in enumerate(zip(sources, kept + (count,)))]
    for copy in copies:
        copy.start()
    center, scale = centered(queries[...])
    query_normed = (center * scale * as_row(gain)).astype(jnp.bfloat16)
    width = queries.shape[1]
    heads = mm(query_normed, w_query[...], NN).astype(jnp.bfloat16)
    put_pairs(heads_out, heads * (1.0 / (width // HEADS) ** 0.5), width // HEADS)
    copies[total].wait()
    live = live_rows(count[0, 0], queries.shape[0])
    live_out[...] = live
    grad_rows = (cot[...].astype(jnp.float32) * live).astype(jnp.bfloat16)
    put_pairs(grad_out, mm(grad_rows, w_out[...], NT).astype(jnp.bfloat16), width // HEADS)
    for copy in copies[:total]:
        copy.wait()


def stage(*refs):
    total = len(refs) // 2
    copies = [pltpu.make_async_copy(refs[k], refs[total + k], refs[-1].at[k]) for k in range(total)]
    for copy in copies:
        copy.start()
    for copy in copies:
        copy.wait()


def pack(*refs):
    at = 0
    for ref in refs[:-1]:
        refs[-1][at : at + ref.shape[0], :] = ref[...]
        at += ref.shape[0]


def join(own, partner, gain, out, mine):
    size = own.shape[0]
    center, scale = centered(jnp.concatenate([own[...], partner[...]], 0))
    normed = (center * scale * as_row(gain)).astype(jnp.bfloat16)
    out[...] = normed
    mine[...] = normed[:size]


def fold(heads, grads, w_key, w_value, heads_back, grads_back):
    lanes = heads.shape[1]
    height = heads.shape[0] * lanes // w_key.shape[1]
    for rows, weight, out in ((heads, w_key, heads_back), (grads, w_value, grads_back)):
        for k in range(w_key.shape[1] // lanes):
            lines = slice(k * height, (k + 1) * height)
            product = mm(rows[lines, :], weight[:, k * lanes : (k + 1) * lanes], NT)
            out[lines, :] = product.astype(out.dtype)


def where_am_i():
    branch = lax.axis_index("branch")
    return branch % 2, (branch >= lax.axis_size("branch") // 2).astype(jnp.int32)


def ordered(first, second):
    core, _ = where_am_i()
    return jnp.where(core == 0, first, second), jnp.where(core == 0, second, first)


def attend(near, normed, kind, heads, grads, heads_back, grads_back, w_key, w_value, probs_out, values_out, scores_out, keys_out):
    keys = mm(normed, w_key[...], NN).astype(jnp.bfloat16)
    values = mm(normed, w_value[...], NN).astype(jnp.bfloat16)
    width = keys.shape[1]
    head = width // HEADS
    rows = kind.shape[1]
    _, volume = where_am_i()
    mine = (kind[...] == 1).astype(jnp.int32) == (volume if near else 1 - volume)
    mine = jnp.concatenate([mine.astype(jnp.int32)] * 2, 1) == 1

    def span(k):
        return slice(2 * head * k, 2 * head * (k + 1))

    def lines(k):
        return slice(2 * rows * k, 2 * rows * (k + 1))

    def products(k):
        return mm(keys[:, span(k)], heads[lines(k), :], NT), mm(values[:, span(k)], grads[lines(k), :], NT)

    def soften(scores, grad_probs):
        expo = jnp.exp(scores - jnp.max(scores, axis=0, keepdims=True))
        total = jnp.sum(expo, axis=0, keepdims=True)
        probs = expo * jnp.where(mine, 1.0 / total, 0.0)
        delta = jnp.sum(grad_probs * probs, axis=0, keepdims=True)
        return probs.astype(jnp.bfloat16), (probs * (grad_probs - delta)).astype(jnp.bfloat16)

    pairs = range(width // (2 * head))
    raw = [products(k) for k in pairs]
    soft = [soften(*x) for x in raw]
    probs, grad_scores = (jnp.concatenate([x[k] for x in soft], 1) for k in (0, 1))
    probs_out[...], values_out[...], scores_out[...], keys_out[...] = probs, values, grad_scores, keys
    return mm(grad_scores, heads_back[...], NN) + mm(probs, grads_back[...], NN)


def row_sums(soft, features):
    width = features.shape[1]
    head, rows = width // HEADS, soft.shape[1] // HEADS
    parts = []
    for k in range(width // (2 * head)):
        x = soft[:, 2 * rows * k : 2 * rows * (k + 1)]
        x = jnp.concatenate([x[:, :rows], x[:, rows:]], 0)
        parts.append(mm(x, masked_pair(features[:, 2 * head * k : 2 * head * (k + 1)], head), TN))
    return jnp.concatenate(parts, 1)


def near_side(counts, kind, heads, grads, heads_back, grads_back, w_key, w_value, chip, *refs):
    both, split, _ = counts
    (got, other), (own_out, send_out, keep_out, *row_outs) = refs[:2], refs[2:]
    pair = chip.shape[0]
    size = pair // 2
    blocks = [chip[...], got[: both * pair, :], other[: both * pair, :]]
    for k in range(both, both + split):
        at = slice(k * pair, (k + 1) * pair)
        blocks.append(ordered(got[at, :], other[at, :])[0])
    grad = attend(True, jnp.concatenate(blocks, 0), kind, heads, grads, heads_back, grads_back, w_key, w_value, *row_outs)
    middle = pair + both * pair
    own_out[...] = grad[:size]
    send_out[:size, :] = grad[size:pair].astype(jnp.bfloat16)
    send_out[size:, :] = grad[middle : middle + both * pair].astype(jnp.bfloat16)
    keep_out[: both * pair, :] = grad[pair:middle]
    keep_out[both * pair :, :] = grad[middle + both * pair :]


def far_side(counts, kind, heads, grads, heads_back, grads_back, w_key, w_value, got, other, got_far, other_far, kept, *refs):
    both, split, far = counts
    send_out, keep_out, *row_outs = refs
    pair = got.shape[0] // (both + split)
    size = pair // 2
    span = far * pair + size
    blocks = [got_far[...], other_far[...]]
    for k in range(both, both + split):
        at = slice(k * pair, (k + 1) * pair)
        blocks.append(ordered(got[at, :], other[at, :])[1])
    grad = attend(False, jnp.concatenate(blocks, 0), kind, heads, grads, heads_back, grads_back, w_key, w_value, *row_outs)
    keep_out[:span, :] = grad[:span]
    send_out[:span, :] = grad[span : 2 * span].astype(jnp.bfloat16)
    here, there = ordered(kept[both * pair :, :], grad[2 * span :])
    keep_out[span:, :] = here
    send_out[span:, :] = there.astype(jnp.bfloat16)


def field_rows(live, queries, near, near_values, far, far_values, w_out, fields):
    mixed = (row_sums(near, near_values) + row_sums(far, far_values)).astype(jnp.bfloat16)
    residual = queries[...].astype(jnp.float32) + mm(mixed, w_out[...], NN)
    fields[...] = (live[...] * residual).astype(jnp.bfloat16)


def query_back(live, queries, cot, near, near_keys, far, far_keys, gain, w_query, query_grad):
    score_scale = 1.0 / (queries.shape[1] // HEADS) ** 0.5
    dq = ((row_sums(near, near_keys) + row_sums(far, far_keys)) * score_scale).astype(jnp.bfloat16)
    center, scale = centered(queries[...])
    back = norm_pullback(center, scale, as_row(gain), mm(dq, w_query[...], NT))
    query_grad[...] = live[...] * (cot[...].astype(jnp.float32) + back)


def add_near(own, keep, got, own_out, *sums):
    size = own.shape[0]
    pair = 2 * size
    own_out[...] = own[...] + got[:size, :].astype(jnp.float32)
    for k, out in enumerate(sums):
        at = k * pair
        out[...] = (keep[at : at + pair, :] + got[size + at : size + at + pair, :].astype(jnp.float32)).astype(out.dtype)


def add_far(keep, got, *sums):
    at = 0
    for out in sums:
        span = slice(at, at + out.shape[0])
        out[...] = (keep[span, :] + got[span, :].astype(jnp.float32)).astype(out.dtype)
        at += out.shape[0]


def add_chips(*refs):
    got, (own, own_out, send_out) = refs[:-3], refs[-3:]
    size = own.shape[0]
    total = got[0][...].astype(jnp.float32)
    for other in got[1:]:
        total = total + other[...].astype(jnp.float32)
    own_out[...] = own[...] + total[:size]
    send_out[...] = total[size:].astype(send_out.dtype)


def anchor_back(anchors, own, got, across, gain, out):
    center, scale = centered(anchors[...])
    grad = own[...] + got[...].astype(jnp.float32) + across[...].astype(jnp.float32)
    out[...] = norm_pullback(center, scale, as_row(gain), grad)


def call(body, outs, *args, staged=(), scratch=()):
    specs = [pl.BlockSpec(memory_space=pltpu.VMEM)] * len(args)
    placed = [pltpu.with_memory_space_constraint(x, pltpu.VMEM) for x in args]
    held = [x if x.size == 1 else pltpu.with_memory_space_constraint(x, pltpu.HBM) for x in staged]
    return pl.pallas_call(
        body,
        out_shape=[pltpu.VMEM(*out) if on_chip else jax.ShapeDtypeStruct(*out) for on_chip, *out in outs],
        in_specs=specs + [pl.BlockSpec(memory_space=pl.ANY if x.size == 1 else pltpu.HBM) for x in staged],
        out_specs=[pl.BlockSpec(memory_space=pltpu.VMEM)] * len(outs),
        scratch_shapes=list(scratch),
        compiler_params=pltpu.CompilerParams(vmem_limit_bytes=32 * 2**20),
    )(*placed, *held)


def exchange_plan(branches, pts):
    top = branches * pts // 2
    nears = [d for d in range(1, top) if not d & pts]
    fars = [d | top for d in nears]
    both = list(zip(nears[:-1:2], nears[1:-1:2]))
    far = list(zip(fars[:-1:2], fars[1:-1:2]))
    return both + [(nears[-1], fars[-1])] + far, (len(both), 1, len(far))


def on_device(sizes, anchors, queries, query_kind, live_count, anchor_gain, query_gain, w_query, w_key, w_value, w_out, cotangent):
    branches, pts = sizes
    group = branches * pts
    plan, counts = exchange_plan(branches, pts)
    both, split, far = counts
    early = both + split

    def send(x, deltas):
        return lax.ppermute(x, GROUP_AXES, [(i, i ^ deltas[(i // pts) % 2]) for i in range(group)])

    def swap(x):
        return send(x, (pts, pts))

    def cross(x):
        return send(x, (group // 2, group // 2))

    size, width = anchors.shape
    rows = queries.shape[0]
    pair = 2 * size
    f32, bf16 = jnp.float32, jnp.bfloat16
    stacked = (HEADS * rows, 2 * width // HEADS)
    partner = swap(anchors)
    needed = (anchors, anchor_gain, queries, cotangent, query_gain, w_query, w_out)
    local, anchor_gain, queries, cotangent, query_gain, w_query, w_out = call(
        stage,
        [(True, x.shape, x.dtype) for x in needed],
        staged=needed,
        scratch=[pltpu.SemaphoreType.DMA((len(needed),))],
    )
    chip, mine = call(join, [(True, (pair, width), bf16), (True, (size, width), bf16)], local, partner, anchor_gain)
    got = []
    for step in plan:
        got.append(send(chip, step))
    across = cross(mine)
    inputs = (w_key, w_value, query_kind.reshape(1, -1))
    heads, grads, live, w_key, w_value, query_kind = call(
        query_side,
        [(True, stacked, bf16)] * 2 + [(True, (rows, 1), f32)] + [(True, x.shape, x.dtype) for x in inputs],
        queries,
        cotangent,
        query_gain,
        w_query,
        w_out,
        staged=inputs + (live_count.reshape(1, 1),),
        scratch=[pltpu.SMEM((1, 1), jnp.int32), pltpu.SemaphoreType.DMA((len(inputs) + 1,))],
    )
    (got_near,) = call(pack, [(True, (pair * early, width), bf16)], *got[:early])
    other_near = swap(got_near)
    got_far = jnp.concatenate([across] + got[early:], 0)
    other_far = swap(got_far)
    folded = [(True, (HEADS * rows, width), bf16)] * 2
    heads_back, grads_back = call(fold, folded, heads, grads, w_key, w_value)
    common = (query_kind, heads, grads, heads_back, grads_back, w_key, w_value)
    half = group * size // 2
    rowwise = [(True, (half, HEADS * rows), bf16), (True, (half, width), bf16)] * 2
    own, send_near, keep_near, probs_near, values_near, scores_near, keys_near = call(
        functools.partial(near_side, counts),
        [(True, (size, width), f32), (True, (size + pair * both, width), bf16), (True, (pair * early, width), f32)] + rowwise,
        *common,
        chip,
        got_near,
        other_near,
    )
    back_near = swap(send_near)
    send_far, keep_far, probs_far, values_far, scores_far, keys_far = call(
        functools.partial(far_side, counts),
        [(True, (size + pair * (far + split), width), bf16), (True, (size + pair * (far + split), width), f32)] + rowwise,
        *common,
        got_near,
        other_near,
        got_far,
        other_far,
        keep_near,
    )
    back_far = swap(send_far)
    own, *sums = call(
        add_near, [(True, (size, width), f32)] + [(True, (pair, width), bf16)] * both, own, keep_near, back_near
    )
    across, *more = call(
        add_far, [(True, (size, width), bf16)] + [(True, (pair, width), bf16)] * (far + split), keep_far, back_far
    )
    sums += more[far:] + more[:far]
    arrived = []
    for part, step in zip(sums, plan):
        arrived.append(send(part, step))
    across = cross(across)
    (fields,) = call(
        field_rows, [(False, (rows, width), bf16)], live, queries, probs_near, values_near, probs_far, values_far, w_out
    )
    (query_grad,) = call(
        query_back, [(False, (rows, width), f32)],
        live, queries, cotangent, scores_near, keys_near, scores_far, keys_far, query_gain, w_query,
    )
    own, last = call(add_chips, [(True, (size, width), f32), (True, (size, width), bf16)], *arrived, own)
    last = swap(last)
    (anchor_grad,) = call(anchor_back, [(True, (size, width), f32)], local, own, last, across, anchor_gain)
    return fields, query_grad, anchor_grad


def solution(mesh):
    split = P(("car",) + GROUP_AXES, None)
    flat = P(("car",) + GROUP_AXES)
    sizes = mesh.shape["branch"], mesh.shape["pts"]

    def body(*args):
        return on_device(sizes, *args)

    return jax.shard_map(
        body,
        mesh=mesh,
        in_specs=(split, split, flat, flat, P(), P(), P(), P(), P(), P(), split),
        out_specs=(split, split, split),
        check_vma=False,
    )
```
